256 devices in a mesh: sec: 16 (over x, y_hi, core), span: 16 (over z, y_lo).
Axes of the slice: x: 4, y: 4 (y_hi: 2, y_lo: 2; y = y_hi * 2 + y_lo), z: 8, core: 2. Of those that a mesh axis runs over, the one named last changes fastest.
Arguments:
- density: float32 [384, 4096], P('sec', 'span'), may hold values from 0.5 to 2
- fields: float32 [4, 384, 4096], P(None, 'sec', 'span'), may hold values from -6 to 6
- bins: int32 [384, 4096], P('sec', 'span'), may hold values from 0 to 127
- owner: int32 [384], P('sec'), may hold values from 0 to 255
- species: float32 [256, 32, 128], P(('sec', 'span')), may hold values from -6 to 6
- rate_matrix: float32 [32, 32], replicated, may hold values from -1 to 1
- inv_weight: float32 [32], replicated, may hold values from 0.5 to 2
- formation: float32 [32], replicated, may hold values from -4 to 4
Outputs:
- species_out: float32 [256, 32, 128], P(('sec', 'span'))
- density_out: float32 [384, 4096], P('sec', 'span')
- fields_out: float32 [4, 384, 4096], P(None, 'sec', 'span')
The draws below stay inside these ranges and needn't reach their ends.
All inputs are finite; a program needn't handle non-finite values.
Results may differ from the reference program's by a relative error of at most 0.0003.
Values sent between devices are 32-bit elements; how exact they have to be, the bound alone decides.
No kernel may reach another device: no remote copies, remote signals or barrier semaphores. Data moves between devices by JAX's collectives and lax.ppermute only.
A program may use at most 64 MiB of HBM per device.

```python
import math
import jax
import jax.numpy as jnp
import numpy as np
from jax import lax

BINS = 128
SPECIES = 32
COUPLING = 2
SECTIONS = 256
COLS = 384
ZSPAN = 4096


def touch_ends(values, stream_key, smallest, high):
    dims = values.shape
    index_at = [jax.random.randint(jax.random.fold_in(stream_key, axis), (), 0, dims[axis]) for axis in range(len(dims))]
    values = values.at[tuple(index_at)].set(smallest)
    longest = dims.index(max(dims))
    index_at[longest] = (index_at[longest] + 1) % dims[longest]
    return values.at[tuple(index_at)].set(high)


def levels(own_key, dims, split, least, top_value):
    loudness = 1.0
    for axis_at, blocks in split:
        steps = jax.random.uniform(jax.random.fold_in(jax.random.fold_in(own_key, 6), axis_at), (blocks,), jnp.float32, least / len(split), top_value / len(split))
        loudness = loudness * jnp.repeat(jnp.exp(steps), dims[axis_at] // blocks).reshape((-1,) + (1,) * (len(dims) - 1 - axis_at))
    return loudness


def cumulative_ranks(number_of, lean):
    portions = [(1 << 20) // math.isqrt(grade ** lean) + 1 for grade in range(1, number_of + 1)]
    scale = 1 + sum(portions) // (1 << 30)
    return np.cumsum(np.array([max(1, weight // scale) for weight in portions]))


def ranked(key, dims, number_of, skew):
    grid = cumulative_ranks(number_of, skew)
    ticket = jax.random.randint(jax.random.fold_in(key, 1), dims, 0, int(grid[number_of - 1]))
    grade = jnp.searchsorted(jnp.asarray(grid, jnp.int32), ticket, side="right")
    return jax.random.permutation(jax.random.fold_in(key, 2), number_of)[grade].astype(jnp.int32)


def bell_draw(key, shape, width, reach, shards=(), kind=jnp.bfloat16):
    drawn = width * jax.random.normal(key, shape, jnp.float32)
    if shards:
        drawn = drawn * levels(key, shape, shards, -0.22, 0.18)
    return jnp.clip(drawn, -reach, reach).astype(kind)


def setup_inputs(seed: int = 0) -> dict:
    keys = jax.random.split(jax.random.key(seed), 9)
    density = jnp.clip(jnp.exp(math.log(2.0) - 1.3862944 * jax.random.uniform(keys[0], (COLS, ZSPAN), jnp.float32) ** levels(keys[0], (COLS, ZSPAN), ((0, 16), (1, 16)), -0.2, 0.2)), 0.5, 2.0)
    fields = bell_draw(keys[1], (4, COLS, ZSPAN), 1.0, 6.0, ((1, 16), (2, 16)), jnp.float32)
    bins = touch_ends(ranked(keys[2], (COLS, ZSPAN), BINS, 2), jax.random.fold_in(keys[2], 3), 0, BINS - 1).astype(jnp.int32)
    owner = touch_ends(ranked(keys[3], (COLS,), SECTIONS, 2), jax.random.fold_in(keys[3], 3), 0, SECTIONS - 1).astype(jnp.int32)
    species = bell_draw(keys[4], (SECTIONS, SPECIES, BINS), 1.0, 6.0, ((0, 256),), jnp.float32)
    rate_matrix = bell_draw(keys[5], (SPECIES, SPECIES), SPECIES ** -0.5, 1.0, (), jnp.float32)
    inv_weight = jnp.clip(jnp.exp(jax.random.uniform(keys[6], (SPECIES,), jnp.float32, math.log(0.5), math.log(2.0))), 0.5, 2.0)
    formation = bell_draw(keys[7], (SPECIES,), 1.0, 4.0, (), jnp.float32)
    return dict(density=density, fields=fields, bins=bins, owner=owner, species=species, rate_matrix=rate_matrix, inv_weight=inv_weight, formation=formation)


def reference(density, fields, bins, owner, species, rate_matrix, inv_weight, formation):
    segment = (owner[:, None] * BINS + bins).reshape(-1)
    eta = (jnp.arange(BINS, dtype=jnp.float32) + 0.5) / BINS
    for step in range(COUPLING):
        values = [density] + [density * fields[k] for k in range(4)]
        sums = jnp.stack([jax.ops.segment_sum(v.reshape(-1), segment, num_segments=SECTIONS * BINS) for v in values])
        sums = sums.reshape(5, SECTIONS, BINS)
        weight = jnp.maximum(sums[0], 1.0)
        cond = sums[1:] / weight[None]
        temp = 1.0 + 4.0 * eta * (1.0 - eta) + 0.5 * jnp.tanh(cond[2])
        rate = jnp.exp(2.0 * (1.0 - 1.0 / temp))
        react = jnp.einsum('ij,sjb->sib', rate_matrix, species, precision=lax.Precision.HIGHEST) * rate[:, None, :]
        padded = jnp.pad(species, ((0, 0), (0, 0), (1, 1)))
        lap = padded[:, :, 2:] + padded[:, :, :-2] - 2.0 * species
        before = jnp.concatenate([jnp.zeros_like(species[:1]), species[:-1]], axis=0)
        mixing = 0.2 * jax.nn.sigmoid(cond[1])
        carry = 0.3 * jax.nn.sigmoid(cond[0])
        species = species + mixing[:, None, :] * lap - carry[:, None, :] * (species - before) + 0.2 * react
        mix = 1.0 + jnp.sum(inv_weight[None, :, None] * species * species, axis=1) / SPECIES
        rho_c = 1.0 / (temp * mix)
        temp_c = temp + 0.1 * jnp.sum(formation[None, :, None] * react, axis=1) - 0.2 * jax.nn.sigmoid(cond[3]) * (temp - 0.5)
        rho_cell = rho_c.reshape(-1)[segment].reshape(density.shape)
        temp_cell = temp_c.reshape(-1)[segment].reshape(density.shape)
        lapz = jnp.roll(fields, 1, axis=2) + jnp.roll(fields, -1, axis=2) - 2.0 * fields
        fields = fields + 0.2 * lapz
        fields = fields.at[2].add(0.3 * (temp_cell - fields[2]))
        density = rho_cell
    return species, density, fields
```

```python
import jax
import jax.numpy as jnp
from jax import lax
from jax.experimental import pallas as pl
from jax.experimental.pallas import tpu as pltpu
from jax.sharding import PartitionSpec as P

F32, BF16 = jnp.float32, jnp.bfloat16
C, Z, NB, NS = 24, 256, 128, 32
G = 16
SECT = 256
LF, LC, LH, LE = 0, 32, 40, 90
LB0, LB1, LOWN = 106, 107, 108
R1 = 32
R2 = C + 3 * G


def iota(shape, dim):
    return lax.broadcasted_iota(jnp.int32, shape, dim)


def parts(value):
    high = value.astype(BF16)
    rest = value - high.astype(F32)
    mid = rest.astype(BF16)
    low = (rest - mid.astype(F32)).astype(BF16)
    return high, mid, low


def column_of(row, n):
    return jnp.sum(jnp.where(iota((n, n), 0) == iota((n, n), 1), row, 0.0), axis=1, keepdims=True)


def sigmoid(x):
    return 0.5 * jnp.tanh(0.5 * x) + 0.5


def dot(a, b, dims):
    return lax.dot_general(a, b, (dims, ((), ())), preferred_element_type=F32)


def bin_kernel(den, fields, bins, owner, species, out, vals, hist, turned, rows):
    lane = iota((C, Z), 1)
    d = den[...]
    vals[0] = d
    vals[5] = jnp.ones((C, Z), F32)
    for k in range(4):
        f = fields[k]
        left = jnp.where(lane == 0, 0.0, pltpu.roll(f, 1, 1))
        right = jnp.where(lane == Z - 1, 0.0, pltpu.roll(f, Z - 1, 1))
        vals[1 + k] = d * f
        vals[6 + k] = f + 0.2 * (left + right - 2.0 * f)
    for q in range(10, 16):
        vals[q] = jnp.zeros((C, Z), F32)
    which = iota((NB, Z), 0)
    for c in range(C):
        hot = jnp.where(which == bins[c : c + 1, :], 1.0, 0.0).astype(BF16)
        full = dot(jnp.concatenate(parts(vals[:, c, :]), axis=0), hot, ((1,), (1,)))
        hist[c] = full[0:16] + full[16:32] + full[32:48]
    lane = iota((C, NB), 1)
    edge = jnp.zeros((C, NB), F32)
    for k in range(4):
        first, last = fields[k, :, 0:NB], fields[k, :, Z - NB : Z]
        for e, (tile, at) in enumerate(((first, 0), (first, 1), (last, NB - 2), (last, NB - 1))):
            to = LE + 4 * e + k
            edge = jnp.where(lane == to, pltpu.roll(tile, (to - at) % NB, 1), edge)
    first, last = bins[:, 0:NB].astype(F32), bins[:, Z - NB : Z].astype(F32)
    edge = jnp.where(lane == LB0, pltpu.roll(first, LB0, 1), edge)
    edge = jnp.where(lane == LB1, pltpu.roll(last, (LB1 + 1) % NB, 1), edge)
    edge = jnp.where(lane == LOWN, column_of(owner[...].astype(F32), C), edge)
    sums = [hist[:, q, :] for q in range(10)]
    turned[0:8, :] = jnp.zeros((8, NB), F32)
    turned[8 + NB : 16 + NB, :] = jnp.zeros((8, NB), F32)
    turned[8 : 8 + NB, :] = jnp.concatenate([species[0], jnp.zeros((NB - NS, NB), F32)], axis=0).T
    packed = turned[pl.ds(6, 33, stride=4), :]
    for a in range(1, 4):
        packed = packed + pltpu.roll(turned[pl.ds(6 + a, 33, stride=4), :], 32 * a, 1)
    rows[0:33, :] = packed
    rows[33:40, :] = jnp.zeros((7, NB), F32)
    for dest in range(G):
        acc = edge
        for k in range(4):
            start = LF + 8 * k
            moved = pltpu.roll(sums[6 + k], (start - 8 * dest) % NB, 1)
            acc = jnp.where((lane >= start) & (lane < start + 8), moved, acc)
        moved = pltpu.roll(sums[5], (LC - 8 * dest) % NB, 1)
        acc = jnp.where((lane >= LC) & (lane < LC + 8), moved, acc)
        for q in range(5):
            start = LH + 10 * q
            moved = pltpu.roll(sums[q], (start - 8 * dest + 1) % NB, 1)
            acc = jnp.where((lane >= start) & (lane < start + 10), moved, acc)
        out[dest, 0:C, :] = acc
        out[dest, C:R1, :] = rows[2 * dest : 2 * dest + 8, :]


def column_kernel(got, out, halo):
    me = lax.axis_index("span")
    lane = iota((C, NB), 1)
    total = got[0, 0:C, :]
    for j in range(1, G):
        total = total + got[j, 0:C, :]
    source, to = iota((NB, 2 * NB), 0), iota((NB, 2 * NB), 1)
    pick = jnp.where(
        to < 32,
        LE + 12 + to // 8,
        jnp.where(
            to < 64,
            LE + (to - 32) // 8,
            jnp.where((to >= 128) & (to < 160), LB0, jnp.where((to >= 160) & (to < 192), LB1, -1)),
        ),
    )
    spread = jnp.where(source == pick, 1.0, 0.0).astype(BF16)
    wide = got[:, 0:C, :].reshape(G * C, NB)
    high, mid, low = parts(wide)
    moved = dot(high, spread, ((1,), (0,))) + dot(mid, spread, ((1,), (0,))) + dot(low, spread, ((1,), (0,)))
    bin_here = (8 * me + lane % 8).astype(F32)
    part = [moved[C * j : C * (j + 1), 0:NB] for j in range(G)]
    fix = jnp.zeros((C, NB), F32)
    for j in range(G):
        beside = jnp.where(lane < 32, part[(j - 1) % G], part[(j + 1) % G])
        fix = fix + jnp.where(moved[C * j : C * (j + 1), NB : 2 * NB] == bin_here, beside, 0.0)
    fix = fix + pltpu.roll(fix, NB - 32, 1)
    total = total + jnp.where(lane < 32, 0.2 * fix, 0.0)
    total = jnp.where(lane >= LE, got[0, 0:C, :], total)
    tiles = [got[:, C + t, :] for t in range(3)]
    for i in range(G):
        out[i, 0:C, :] = total
        for t in range(3):
            out[i, C + G * t : C + G * (t + 1), :] = tiles[t]
    halo[0] = got[lax.rem(me + G - 1, G), 0:C, :]
    halo[1] = got[lax.rem(me + 1, G), 0:C, :]


def section_kernel(got, rate_matrix, inv_weight, formation, out, sums, turned):
    row_at, me = lax.axis_index("sec"), lax.axis_index("span")
    wide = got[:, 0:C, :].reshape(G * C, NB)
    section = iota((G * C, SECT), 1).astype(F32)
    hot = jnp.where(wide[:, LOWN : LOWN + 1] == section, 1.0, 0.0).astype(BF16)
    full = dot(jnp.concatenate(parts(wide.T), axis=0), hot, ((1,), (0,)))
    sums[...] = full[0:NB] + full[NB : 2 * NB] + full[2 * NB : 3 * NB]
    weights = column_of(inv_weight[...], NS)
    heats = column_of(formation[...], NS)
    block = jnp.concatenate([rate_matrix[...]] * 4, axis=1)
    block = jnp.concatenate([block] * 4, axis=0)
    block = jnp.where(iota((NB, NB), 0) // NS == iota((NB, NB), 1) // NS, block, 0.0)
    first_lane = iota((NS, SECT), 1) == 0

    def rates(tile):
        return jnp.dot(block, tile, precision=lax.Precision.HIGHEST, preferred_element_type=F32)

    def advance(density, moments, bin_at, current, reaction):
        n = density.shape[0]
        weight = jnp.maximum(density, 1.0)
        cond = [m / weight for m in moments]
        eta = ((bin_at + iota((n, SECT), 0)).astype(F32) + 0.5) / NB
        temp = 1.0 + 4.0 * eta * (1.0 - eta) + 0.5 * jnp.tanh(cond[2])
        rate = jnp.exp(2.0 * (1.0 - 1.0 / temp))
        mixing = 0.2 * sigmoid(cond[1])
        carried = 0.3 * sigmoid(cond[0])
        updated, mixes, released = [], [], []
        for r in range(n):
            here = current[r + 1]
            before = jnp.where(first_lane, 0.0, pltpu.roll(here, 1, 1))
            react = reaction[r] * rate[r : r + 1]
            new = (
                here
                + mixing[r : r + 1] * (current[r + 2] + current[r] - 2.0 * here)
                - carried[r : r + 1] * (here - before)
                + 0.2 * react
            )
            updated.append(new)
            mixes.append(jnp.sum(weights * new * new, axis=0, keepdims=True))
            released.append(jnp.sum(heats * react, axis=0, keepdims=True))
        mix = 1.0 + jnp.concatenate(mixes, axis=0) / NS
        rho = 1.0 / (temp * mix)
        temp_c = temp + 0.1 * jnp.concatenate(released, axis=0) - 0.2 * sigmoid(cond[3]) * (temp - 0.5)
        return updated, rho, temp_c

    tiles = [got[:, C + G * t : C + G * (t + 1), :].reshape(SECT, NB).T for t in range(3)]
    reacts = [rates(tile) for tile in tiles]
    current = [tiles[b // 4][NS * (b % 4) : NS * (b % 4 + 1)] for b in range(12)]
    reaction = [reacts[b // 4][NS * (b % 4) : NS * (b % 4 + 1)] for b in range(1, 11)]
    first = [sums[LH + 10 * q : LH + 10 * (q + 1), :] for q in range(5)]
    updated, rho, temp0 = advance(first[0], first[1:], 8 * me - 1, current, reaction)
    updated[0] = jnp.where(me == 0, 0.0, updated[0])
    updated[9] = jnp.where(me == G - 1, 0.0, updated[9])
    rho, temp0 = rho[1:9], temp0[1:9]
    count = sums[LC : LC + 8, :]
    moments = [rho * sums[LF + 8 * k : LF + 8 * k + 8, :] for k in range(4)]
    moments[2] = 0.7 * moments[2] + 0.3 * rho * temp0 * count
    reacts = [rates(jnp.concatenate(updated[1 + 4 * t : 5 + 4 * t], axis=0)) for t in range(2)]
    reaction = [reacts[b // 4][NS * (b % 4) : NS * (b % 4 + 1)] for b in range(8)]
    final, rho, temp1 = advance(rho * count, moments, 8 * me, updated, reaction)

    own = got[row_at, 0:C, LOWN : LOWN + 1]
    own = jnp.concatenate([own] * 3 + [jnp.full((NB - 3 * C, 1), -1.0, F32)], axis=0)
    hot = jnp.where(own == iota((NB, SECT), 1).astype(F32), 1.0, 0.0).astype(BF16)
    table = jnp.concatenate([temp0, temp1, rho], axis=0)
    full = dot(jnp.concatenate(parts(table), axis=0), hot, ((1,), (1,)))
    full = full[0:24] + full[24:48] + full[48:72]
    lane = iota((8, NB), 1)
    cells = jnp.where(lane < C, full[0:8], jnp.where(lane < 2 * C, full[8:16], full[16:24]))
    for t in range(2):
        tile = jnp.concatenate(final[4 * t : 4 * t + 4], axis=0)
        turned[t] = jnp.where(row_at < 8, tile[:, 0:NB], tile[:, NB:SECT]).T
    lane = iota((G, NB), 1)
    start = pl.multiple_of(16 * lax.rem(row_at, 8), 16)
    for b in range(8):
        own_sections = turned[b // 4, pl.ds(start, G), :]
        moved = pltpu.roll(own_sections, (96 - 32 * (b % 4)) % NB, 1)
        out[:, b, :] = jnp.where(lane >= 96, moved, cells[b : b + 1, :])


def cell_kernel(got, halo, fields, bins, species_out, density_out, fields_out):
    table = got[...].reshape(NB, NB).T
    species_out[0] = table[96:128]
    temp0, temp1, rho = table[0:C], table[C : 2 * C], table[2 * C : 3 * C]

    def look(tab, index):
        return jnp.take_along_axis(tab, index, axis=1)

    def cells(tab):
        return jnp.concatenate([look(tab, bins[:, 0:NB]), look(tab, bins[:, NB:Z])], axis=1)

    density_out[...] = cells(rho)
    lane = iota((C, Z), 1)
    left, right = halo[0], halo[1]

    def shifted(f, before, after):
        return jnp.where(lane == 0, before, pltpu.roll(f, 1, 1)) + jnp.where(
            lane == Z - 1, after, pltpu.roll(f, Z - 1, 1)
        )

    for k in range(4):
        f = fields[k]
        l1, l2 = left[:, LE + 12 + k : LE + 13 + k], left[:, LE + 8 + k : LE + 9 + k]
        r1, r2 = right[:, LE + k : LE + 1 + k], right[:, LE + 4 + k : LE + 5 + k]
        new = f + 0.2 * (shifted(f, l1, r1) - 2.0 * f)
        new_l = l1 + 0.2 * (l2 + f[:, 0:1] - 2.0 * l1)
        new_r = r1 + 0.2 * (f[:, Z - 1 : Z] + r2 - 2.0 * r1)
        if k == 2:
            new = new + 0.3 * (cells(temp0) - new)
            at_l = jnp.broadcast_to(left[:, LB1 : LB1 + 1].astype(jnp.int32), (C, NB))
            at_r = jnp.broadcast_to(right[:, LB0 : LB0 + 1].astype(jnp.int32), (C, NB))
            new_l = new_l + 0.3 * (look(temp0, at_l)[:, 0:1] - new_l)
            new_r = new_r + 0.3 * (look(temp0, at_r)[:, 0:1] - new_r)
        new = new + 0.2 * (shifted(new, new_l, new_r) - 2.0 * new)
        if k == 2:
            new = new + 0.3 * (cells(temp1) - new)
        fields_out[k] = new


def call(kernel, name, outs, ins, scratch=()):
    space = pl.BlockSpec(memory_space=pltpu.VMEM)
    shapes = [jax.ShapeDtypeStruct(s, F32) for s in outs]
    return pl.pallas_call(
        kernel,
        name=name,
        out_shape=shapes,
        in_specs=[space] * len(ins),
        out_specs=[space] * len(outs),
        scratch_shapes=[pltpu.VMEM(s, F32) for s in scratch],
    )(*ins)


def body(density, fields, bins, owner, species, rate_matrix, inv_weight, formation):
    (sent,) = call(
        bin_kernel,
        "bin",
        [(G, R1, NB)],
        [density, fields, bins, owner.reshape(1, C), species],
        [(16, C, Z), (C, 16, NB), (16 + NB, NB), (40, NB)],
    )
    got = lax.all_to_all(sent, "span", 0, 0, tiled=True)
    sent, halo = call(column_kernel, "column", [(G, R2, NB), (2, C, NB)], [got])
    got = lax.all_to_all(sent, "sec", 0, 0, tiled=True)
    (sent,) = call(
        section_kernel,
        "section",
        [(G, 8, NB)],
        [got, rate_matrix, inv_weight.reshape(1, NS), formation.reshape(1, NS)],
        [(NB, SECT), (2, NB, NB)],
    )
    got = lax.all_to_all(sent, "span", 0, 0, tiled=True)
    return call(
        cell_kernel,
        "cell",
        [(1, NS, NB), (C, Z), (4, C, Z)],
        [got, halo, fields, bins],
    )


def solution(mesh):
    return jax.shard_map(
        lambda *args: tuple(body(*args)),
        mesh=mesh,
        in_specs=(
            P("sec", "span"),
            P(None, "sec", "span"),
            P("sec", "span"),
            P("sec"),
            P(("sec", "span"), None, None),
            P(),
            P(),
            P(),
        ),
        out_specs=(P(("sec", "span"), None, None), P("sec", "span"), P(None, "sec", "span")),
        check_vma=False,
    )
```

```python
import jax
import jax.numpy as jnp
from jax import lax
from jax.experimental import pallas as pl
from jax.experimental.pallas import tpu as pltpu
from jax.sharding import PartitionSpec as P

F32, BF16 = jnp.float32, jnp.bfloat16
C, Z, NB, NS = 24, 256, 128, 32
G = 16
SECT = 256
LF, LC, LH, LE = 0, 32, 40, 90
LB0, LB1, LOWN = 106, 107, 108
LS = 112
R2 = C + 3 * G


def iota(shape, dim):
    return lax.broadcasted_iota(jnp.int32, shape, dim)


def parts(value):
    high = value.astype(BF16)
    rest = value - high.astype(F32)
    mid = rest.astype(BF16)
    low = (rest - mid.astype(F32)).astype(BF16)
    return high, mid, low


def column_of(row, n):
    return jnp.sum(jnp.where(iota((n, n), 0) == iota((n, n), 1), row, 0.0), axis=1, keepdims=True)


def sigmoid(x):
    return 0.5 * jnp.tanh(0.5 * x) + 0.5


def dot(a, b, dims):
    return lax.dot_general(a, b, (dims, ((), ())), preferred_element_type=F32)


def bin_kernel(*refs):
    out, vals, hist, rows = refs[5:9]
    den, fields, bins, owner, species = refs[9:14]
    copies = [pltpu.make_async_copy(refs[n], refs[9 + n], refs[14].at[n]) for n in range(5)]
    for copy in copies:
        copy.start()
    for copy in copies:
        copy.wait()
    lane = iota((C, Z), 1)
    d = den[...]
    vals[0] = d
    vals[5] = jnp.ones((C, Z), F32)
    for k in range(4):
        f = fields[k]
        left = jnp.where(lane == 0, 0.0, pltpu.roll(f, 1, 1))
        right = jnp.where(lane == Z - 1, 0.0, pltpu.roll(f, Z - 1, 1))
        vals[1 + k] = d * f
        vals[6 + k] = f + 0.2 * (left + right - 2.0 * f)
    for q in range(10, 16):
        vals[q] = jnp.zeros((C, Z), F32)
    which = iota((NB, Z), 0)
    for c in range(C):
        hot = jnp.where(which == bins[c : c + 1, :], 1.0, 0.0).astype(BF16)
        full = dot(jnp.concatenate(parts(vals[:, c, :]), axis=0), hot, ((1,), (1,)))
        hist[c] = full[0:16] + full[16:32] + full[32:48]
    lane = iota((C, NB), 1)
    edge = jnp.zeros((C, NB), F32)
    for k in range(4):
        first, last = fields[k, :, 0:NB], fields[k, :, Z - NB : Z]
        for e, (tile, at) in enumerate(((first, 0), (first, 1), (last, NB - 2), (last, NB - 1))):
            to = LE + 4 * e + k
            edge = jnp.where(lane == to, pltpu.roll(tile, (to - at) % NB, 1), edge)
    first, last = bins[:, 0:NB].astype(F32), bins[:, Z - NB : Z].astype(F32)
    edge = jnp.where(lane == LB0, pltpu.roll(first, LB0, 1), edge)
    edge = jnp.where(lane == LB1, pltpu.roll(last, (LB1 + 1) % NB, 1), edge)
    edge = jnp.where(lane == LOWN, column_of(owner[...].astype(F32), C), edge)
    sums = [hist[:, q, :] for q in range(10)]
    turned = jnp.concatenate([species[0], jnp.zeros((NB - NS, NB), F32)], axis=0).T
    rows[0:8, :] = jnp.zeros((8, NB), F32)
    rows[256:264, :] = jnp.zeros((8, NB), F32)
    rows[pl.ds(4, NB, stride=2), :] = pltpu.roll(turned, LS, 1)
    rows[pl.ds(5, NB, stride=2), :] = pltpu.roll(turned, LS - 16, 1)
    for dest in range(G):
        acc = jnp.where(lane >= LS, rows[16 * dest : 16 * dest + C, :], edge)
        for k in range(4):
            start = LF + 8 * k
            moved = pltpu.roll(sums[6 + k], (start - 8 * dest) % NB, 1)
            acc = jnp.where((lane >= start) & (lane < start + 8), moved, acc)
        moved = pltpu.roll(sums[5], (LC - 8 * dest) % NB, 1)
        acc = jnp.where((lane >= LC) & (lane < LC + 8), moved, acc)
        for q in range(5):
            start = LH + 10 * q
            moved = pltpu.roll(sums[q], (start - 8 * dest + 1) % NB, 1)
            acc = jnp.where((lane >= start) & (lane < start + 10), moved, acc)
        out[dest] = acc


def column_kernel(got, out, halo):
    me = lax.axis_index("span")
    lane = iota((C, NB), 1)
    total = got[0, 0:C, :]
    for j in range(1, G):
        total = total + got[j, 0:C, :]
    source, to = iota((NB, 2 * NB), 0), iota((NB, 2 * NB), 1)
    pick = jnp.where(
        to < 32,
        LE + 12 + to // 8,
        jnp.where(
            to < 64,
            LE + (to - 32) // 8,
            jnp.where((to >= 128) & (to < 160), LB0, jnp.where((to >= 160) & (to < 192), LB1, -1)),
        ),
    )
    spread = jnp.where(source == pick, 1.0, 0.0).astype(BF16)
    wide = got[:, 0:C, :].reshape(G * C, NB)
    high, mid, low = parts(wide)
    moved = dot(high, spread, ((1,), (0,))) + dot(mid, spread, ((1,), (0,))) + dot(low, spread, ((1,), (0,)))
    bin_here = (8 * me + lane % 8).astype(F32)
    part = [moved[C * j : C * (j + 1), 0:NB] for j in range(G)]
    fix = jnp.zeros((C, NB), F32)
    for j in range(G):
        beside = jnp.where(lane < 32, part[(j - 1) % G], part[(j + 1) % G])
        fix = fix + jnp.where(moved[C * j : C * (j + 1), NB : 2 * NB] == bin_here, beside, 0.0)
    fix = fix + pltpu.roll(fix, NB - 32, 1)
    total = total + jnp.where(lane < 32, 0.2 * fix, 0.0)
    total = jnp.where(lane >= LE, got[0, 0:C, :], total)
    lane = iota((G, NB), 1)
    tiles = []
    for t in range(3):
        tile = jnp.zeros((G, NB), F32)
        for p in range(8):
            moved = pltpu.roll(got[:, 8 * t + p, :], (16 * p - LS) % NB, 1)
            tile = jnp.where((lane >= 16 * p) & (lane < 16 * p + 16), moved, tile)
        tiles.append(tile)
    for i in range(G // 2):
        out[i, 0:C, :] = total
        for t in range(3):
            out[i, C + G * t : C + G * (t + 1), :] = tiles[t]
    halo[0] = got[lax.rem(me + G - 1, G), 0:C, :]
    halo[1] = got[lax.rem(me + 1, G), 0:C, :]


def section_kernel(got, other, rate_matrix, inv_weight, formation, out, sums, turned):
    row_at, me = lax.axis_index("sec"), lax.axis_index("span")
    half = G // 2 * C
    wide = jnp.concatenate([got[:, 0:C, :].reshape(half, NB), other[:, 0:C, :].reshape(half, NB)], axis=0)
    section = iota((G * C, SECT), 1).astype(F32)
    hot = jnp.where(wide[:, LOWN : LOWN + 1] == section, 1.0, 0.0).astype(BF16)
    full = dot(jnp.concatenate(parts(wide.T), axis=0), hot, ((1,), (0,)))
    sums[...] = full[0:NB] + full[NB : 2 * NB] + full[2 * NB : 3 * NB]
    weights = column_of(inv_weight[...], NS)
    heats = column_of(formation[...], NS)
    block = jnp.concatenate([rate_matrix[...]] * 4, axis=1)
    block = jnp.concatenate([block] * 4, axis=0)
    block = jnp.where(iota((NB, NB), 0) // NS == iota((NB, NB), 1) // NS, block, 0.0)
    first_lane = iota((NS, SECT), 1) == 0

    def rates(tile):
        return jnp.dot(block, tile, precision=lax.Precision.HIGHEST, preferred_element_type=F32)

    def advance(density, moments, bin_at, current, reaction):
        n = density.shape[0]
        weight = jnp.maximum(density, 1.0)
        cond = [m / weight for m in moments]
        eta = ((bin_at + iota((n, SECT), 0)).astype(F32) + 0.5) / NB
        temp = 1.0 + 4.0 * eta * (1.0 - eta) + 0.5 * jnp.tanh(cond[2])
        rate = jnp.exp(2.0 * (1.0 - 1.0 / temp))
        mixing = 0.2 * sigmoid(cond[1])
        carried = 0.3 * sigmoid(cond[0])
        updated, mixes, released = [], [], []
        for r in range(n):
            here = current[r + 1]
            before = jnp.where(first_lane, 0.0, pltpu.roll(here, 1, 1))
            react = reaction[r] * rate[r : r + 1]
            new = (
                here
                + mixing[r : r + 1] * (current[r + 2] + current[r] - 2.0 * here)
                - carried[r : r + 1] * (here - before)
                + 0.2 * react
            )
            updated.append(new)
            mixes.append(jnp.sum(weights * new * new, axis=0, keepdims=True))
            released.append(jnp.sum(heats * react, axis=0, keepdims=True))
        mix = 1.0 + jnp.concatenate(mixes, axis=0) / NS
        rho = 1.0 / (temp * mix)
        temp_c = temp + 0.1 * jnp.concatenate(released, axis=0) - 0.2 * sigmoid(cond[3]) * (temp - 0.5)
        return updated, rho, temp_c

    even = lax.rem(row_at, 2) == 0
    tiles = []
    for t in range(3):
        span = slice(C + G * t, C + G * (t + 1))
        tile = []
        for i in range(G):
            mine, theirs = got[i // 2, span, :], other[i // 2, span, :]
            tile.append(jnp.where(even, mine, theirs) if i % 2 == 0 else jnp.where(even, theirs, mine))
        tiles.append(jnp.concatenate(tile, axis=0).T)
    reacts = [rates(tile) for tile in tiles]
    current = [tiles[b // 4][NS * (b % 4) : NS * (b % 4 + 1)] for b in range(12)]
    reaction = [reacts[b // 4][NS * (b % 4) : NS * (b % 4 + 1)] for b in range(1, 11)]
    first = [sums[LH + 10 * q : LH + 10 * (q + 1), :] for q in range(5)]
    updated, rho, temp0 = advance(first[0], first[1:], 8 * me - 1, current, reaction)
    updated[0] = jnp.where(me == 0, 0.0, updated[0])
    updated[9] = jnp.where(me == G - 1, 0.0, updated[9])
    rho, temp0 = rho[1:9], temp0[1:9]
    count = sums[LC : LC + 8, :]
    moments = [rho * sums[LF + 8 * k : LF + 8 * k + 8, :] for k in range(4)]
    moments[2] = 0.7 * moments[2] + 0.3 * rho * temp0 * count
    reacts = [rates(jnp.concatenate(updated[1 + 4 * t : 5 + 4 * t], axis=0)) for t in range(2)]
    reaction = [reacts[b // 4][NS * (b % 4) : NS * (b % 4 + 1)] for b in range(8)]
    final, rho, temp1 = advance(rho * count, moments, 8 * me, updated, reaction)

    own = got[row_at // 2, 0:C, LOWN : LOWN + 1]
    own = jnp.concatenate([own] * 3 + [jnp.full((NB - 3 * C, 1), -1.0, F32)], axis=0)
    hot = jnp.where(own == iota((NB, SECT), 1).astype(F32), 1.0, 0.0).astype(BF16)
    table = jnp.concatenate([temp0, temp1, rho], axis=0)
    full = dot(jnp.concatenate(parts(table), axis=0), hot, ((1,), (1,)))
    full = full[0:24] + full[24:48] + full[48:72]
    lane = iota((8, NB), 1)
    cells = jnp.where(lane < C, full[0:8], jnp.where(lane < 2 * C, full[8:16], full[16:24]))
    for t in range(2):
        tile = jnp.concatenate(final[4 * t : 4 * t + 4], axis=0)
        turned[t] = jnp.where(row_at < 8, tile[:, 0:NB], tile[:, NB:SECT]).T
    lane = iota((G, NB), 1)
    start = pl.multiple_of(16 * lax.rem(row_at, 8), 16)
    for b in range(8):
        own_sections = turned[b // 4, pl.ds(start, G), :]
        moved = pltpu.roll(own_sections, (96 - 32 * (b % 4)) % NB, 1)
        out[:, b, :] = jnp.where(lane >= 96, moved, cells[b : b + 1, :])


def cell_kernel(got, halo, fields, bins, species_out, density_out, fields_out):
    table = got[...].reshape(NB, NB).T
    species_out[0] = table[96:128]
    temp0, temp1, rho = table[0:C], table[C : 2 * C], table[2 * C : 3 * C]

    def look(tab, index):
        return jnp.take_along_axis(tab, index, axis=1)

    def cells(tab):
        return jnp.concatenate([look(tab, bins[:, 0:NB]), look(tab, bins[:, NB:Z])], axis=1)

    density_out[...] = cells(rho)
    lane = iota((C, Z), 1)
    left, right = halo[0], halo[1]

    def shifted(f, before, after):
        return jnp.where(lane == 0, before, pltpu.roll(f, 1, 1)) + jnp.where(
            lane == Z - 1, after, pltpu.roll(f, Z - 1, 1)
        )

    for k in range(4):
        f = fields[k]
        l1, l2 = left[:, LE + 12 + k : LE + 13 + k], left[:, LE + 8 + k : LE + 9 + k]
        r1, r2 = right[:, LE + k : LE + 1 + k], right[:, LE + 4 + k : LE + 5 + k]
        new = f + 0.2 * (shifted(f, l1, r1) - 2.0 * f)
        new_l = l1 + 0.2 * (l2 + f[:, 0:1] - 2.0 * l1)
        new_r = r1 + 0.2 * (f[:, Z - 1 : Z] + r2 - 2.0 * r1)
        if k == 2:
            new = new + 0.3 * (cells(temp0) - new)
            at_l = jnp.broadcast_to(left[:, LB1 : LB1 + 1].astype(jnp.int32), (C, NB))
            at_r = jnp.broadcast_to(right[:, LB0 : LB0 + 1].astype(jnp.int32), (C, NB))
            new_l = new_l + 0.3 * (look(temp0, at_l)[:, 0:1] - new_l)
            new_r = new_r + 0.3 * (look(temp0, at_r)[:, 0:1] - new_r)
        new = new + 0.2 * (shifted(new, new_l, new_r) - 2.0 * new)
        if k == 2:
            new = new + 0.3 * (cells(temp1) - new)
        fields_out[k] = new


def call(kernel, name, outs, ins, scratch=(), space=pltpu.VMEM):
    return pl.pallas_call(
        kernel,
        name=name,
        out_shape=[jax.ShapeDtypeStruct(s, F32) for s in outs],
        in_specs=[pl.BlockSpec(memory_space=space)] * len(ins),
        out_specs=[pl.BlockSpec(memory_space=pltpu.VMEM)] * len(outs),
        scratch_shapes=[pltpu.VMEM(s, F32) if isinstance(s, tuple) else s for s in scratch],
        compiler_params=pltpu.CompilerParams(vmem_limit_bytes=16 << 20),
    )(*ins)


def body(density, fields, bins, owner, species, rate_matrix, inv_weight, formation):
    ins = [density, fields, bins, owner.reshape(1, C), species]
    scratch = [(16, C, Z), (C, 16, NB), (264, NB)]
    scratch += [pltpu.VMEM(x.shape, x.dtype) for x in ins] + [pltpu.SemaphoreType.DMA((5,))]
    (sent,) = call(bin_kernel, "bin", [(G, C, NB)], ins, scratch, pltpu.HBM)
    got = lax.all_to_all(sent, "span", 0, 0, tiled=True)
    sent, halo = call(column_kernel, "column", [(G // 2, R2, NB), (2, C, NB)], [got])
    groups = [list(range(core, G, 2)) for core in range(2)]
    got = lax.all_to_all(sent, "sec", 0, 0, axis_index_groups=groups, tiled=True)
    other = lax.ppermute(got, "sec", [(i, i ^ 1) for i in range(G)])
    (sent,) = call(
        section_kernel,
        "section",
        [(G, 8, NB)],
        [got, other, rate_matrix, inv_weight.reshape(1, NS), formation.reshape(1, NS)],
        [(NB, SECT), (2, NB, NB)],
    )
    got = lax.all_to_all(sent, "span", 0, 0, tiled=True)
    return call(
        cell_kernel,
        "cell",
        [(1, NS, NB), (C, Z), (4, C, Z)],
        [got, halo, fields, bins],
    )


def solution(mesh):
    return jax.shard_map(
        lambda *args: tuple(body(*args)),
        mesh=mesh,
        in_specs=(
            P("sec", "span"),
            P(None, "sec", "span"),
            P("sec", "span"),
            P("sec"),
            P(("sec", "span"), None, None),
            P(),
            P(),
            P(),
        ),
        out_specs=(P(("sec", "span"), None, None), P("sec", "span"), P(None, "sec", "span")),
        check_vma=False,
    )
```

```python
import jax
import jax.numpy as jnp
from jax import lax
from jax.experimental import pallas as pl
from jax.experimental.pallas import tpu as pltpu
from jax.sharding import PartitionSpec as P

F32, BF16 = jnp.float32, jnp.bfloat16
C, Z, NB, NS = 24, 256, 128, 32
G = 16
SECT = 256
LF, LC, LH, LE = 0, 32, 40, 90
LB0, LB1, LOWN = 106, 107, 108
LS = 112
R2 = C + 3 * G


def iota(shape, dim):
    return lax.broadcasted_iota(jnp.int32, shape, dim)


def parts(value):
    high = value.astype(BF16)
    rest = value - high.astype(F32)
    mid = rest.astype(BF16)
    low = (rest - mid.astype(F32)).astype(BF16)
    return high, mid, low


def column_of(row, n):
    return jnp.sum(jnp.where(iota((n, n), 0) == iota((n, n), 1), row, 0.0), axis=1, keepdims=True)


def sigmoid(x):
    return 0.5 * jnp.tanh(0.5 * x) + 0.5


def dot(a, b, dims):
    return lax.dot_general(a, b, (dims, ((), ())), preferred_element_type=F32)


def bin_kernel(*refs):
    ins, (sent, consts), held = refs[0:8], refs[8:10], refs[10:18]
    vals, hist, rows, labels, out, shared, arrived, left = refs[18:26]
    bins, fields, den, species, owner, rate_matrix, inv_weight, formation = held
    copies = [pltpu.make_async_copy(ins[n], held[n], arrived.at[n]) for n in range(8)]
    for copy in copies:
        copy.start()
    for copy in copies:
        copy.wait()
    lane = iota((NS, NB), 1)
    block = jnp.concatenate([rate_matrix[...], jnp.zeros((NS, NB - NS), F32)], axis=1)
    block = jnp.where(lane == NS, column_of(inv_weight[...], NS), block)
    shared[...] = jnp.where(lane == NS + 1, column_of(formation[...], NS), block)
    leaving = [pltpu.make_async_copy(shared, consts, left.at[G])]
    leaving[0].start()
    lane = iota((C, Z), 1)
    d = den[...]

    def keep(q, value):
        high, mid, low = parts(value)
        for p, part in enumerate((high, mid, low)):
            at = C * (16 * p + q)
            part = part.astype(F32)
            vals[0, at : at + C, :] = part[:, 0:NB]
            vals[1, at : at + C, :] = part[:, NB:Z]

    keep(0, d)
    keep(5, jnp.ones((C, Z), F32))
    for k in range(4):
        f = fields[k]
        before = jnp.where(lane == 0, 0.0, pltpu.roll(f, 1, 1))
        after = jnp.where(lane == Z - 1, 0.0, pltpu.roll(f, Z - 1, 1))
        keep(1 + k, d * f)
        keep(6 + k, f + 0.2 * (before + after - 2.0 * f))
    for p in range(3):
        at = C * (16 * p + 10)
        for h in range(2):
            vals[h, at : at + 6 * C, :] = jnp.zeros((6 * C, NB), F32)
    labels[...] = bins[...].astype(F32)
    which = iota((NB, Z), 0).astype(F32).astype(BF16).reshape(8, 16, Z)
    one, zero = jnp.ones((8, 16, Z), BF16), jnp.zeros((8, 16, Z), BF16)
    for c in range(C):
        label = jnp.broadcast_to(labels[c : c + 1, :], (16, Z)).astype(BF16)
        hot = jnp.where(which == label[None], one, zero).reshape(NB, Z)
        cells = [vals[h, pl.ds(c, 48, stride=C), :] for h in range(2)]
        full = dot(jnp.concatenate(cells, axis=1).astype(BF16), hot, ((1,), (1,)))
        hist[16 * c : 16 * c + 16, :] = full[0:16] + full[16:32] + full[32:48]
    lane = iota((C, NB), 1)
    edge = jnp.zeros((C, NB), F32)
    for k in range(4):
        first, last = fields[k, :, 0:NB], fields[k, :, Z - NB : Z]
        for e, (tile, at) in enumerate(((first, 0), (first, 1), (last, NB - 2), (last, NB - 1))):
            to = LE + 4 * e + k
            edge = jnp.where(lane == to, pltpu.roll(tile, (to - at) % NB, 1), edge)
    first, last = labels[:, 0:NB], labels[:, Z - NB : Z]
    edge = jnp.where(lane == LB0, pltpu.roll(first, LB0, 1), edge)
    edge = jnp.where(lane == LB1, pltpu.roll(last, (LB1 + 1) % NB, 1), edge)
    edge = jnp.where(lane == LOWN, column_of(owner[...].astype(F32), C), edge)
    sums = [hist[pl.ds(q, C, stride=16), :] for q in range(10)]
    turned = jnp.concatenate([species[0], jnp.zeros((NB - NS, NB), F32)], axis=0).T
    rows[0:8, :] = jnp.zeros((8, NB), F32)
    rows[256:264, :] = jnp.zeros((8, NB), F32)
    rows[pl.ds(4, NB, stride=2), :] = pltpu.roll(turned, LS, 1)
    rows[pl.ds(5, NB, stride=2), :] = pltpu.roll(turned, LS - 16, 1)
    for dest in range(G):
        acc = jnp.where(lane >= LS, rows[16 * dest : 16 * dest + C, :], edge)
        for k in range(4):
            start = LF + 8 * k
            moved = pltpu.roll(sums[6 + k], (start - 8 * dest) % NB, 1)
            acc = jnp.where((lane >= start) & (lane < start + 8), moved, acc)
        moved = pltpu.roll(sums[5], (LC - 8 * dest) % NB, 1)
        acc = jnp.where((lane >= LC) & (lane < LC + 8), moved, acc)
        for q in range(5):
            start = LH + 10 * q
            moved = pltpu.roll(sums[q], (start - 8 * dest + 1) % NB, 1)
            acc = jnp.where((lane >= start) & (lane < start + 10), moved, acc)
        out[dest] = acc
        leaving.append(pltpu.make_async_copy(out.at[dest], sent.at[dest], left.at[dest]))
        leaving[-1].start()
    for copy in leaving:
        copy.wait()


def column_kernel(got, out, halo):
    me = lax.axis_index("span")
    lane = iota((C, NB), 1)
    total = got[0:C, :]
    for j in range(1, G):
        total = total + got[C * j : C * (j + 1), :]
    source, to = iota((NB, 2 * NB), 0), iota((NB, 2 * NB), 1)
    pick = jnp.where(
        to < 32,
        LE + 12 + to // 8,
        jnp.where(
            to < 64,
            LE + (to - 32) // 8,
            jnp.where((to >= 128) & (to < 160), LB0, jnp.where((to >= 160) & (to < 192), LB1, -1)),
        ),
    )
    spread = jnp.where(source == pick, 1.0, 0.0).astype(BF16)
    high, mid, low = parts(got[...])
    moved = dot(high, spread, ((1,), (0,))) + dot(mid, spread, ((1,), (0,))) + dot(low, spread, ((1,), (0,)))
    bin_here = (8 * me + lane % 8).astype(F32)
    part = [moved[C * j : C * (j + 1), 0:NB] for j in range(G)]
    fix = jnp.zeros((C, NB), F32)
    for j in range(G):
        beside = jnp.where(lane < 32, part[(j - 1) % G], part[(j + 1) % G])
        fix = fix + jnp.where(moved[C * j : C * (j + 1), NB : 2 * NB] == bin_here, beside, 0.0)
    fix = fix + pltpu.roll(fix, NB - 32, 1)
    total = total + jnp.where(lane < 32, 0.2 * fix, 0.0)
    total = jnp.where(lane >= LE, got[0:C, :], total)
    lane = iota((G, NB), 1)
    tiles = []
    for t in range(3):
        tile = jnp.zeros((G, NB), F32)
        for p in range(8):
            moved = pltpu.roll(got[pl.ds(8 * t + p, G, stride=C), :], (16 * p - LS) % NB, 1)
            tile = jnp.where((lane >= 16 * p) & (lane < 16 * p + 16), moved, tile)
        tiles.append(tile)
    for i in range(G // 2):
        out[i, 0:C, :] = total
        for t in range(3):
            out[i, C + G * t : C + G * (t + 1), :] = tiles[t]
    halo[0] = got[pl.ds(pl.multiple_of(C * lax.rem(me + G - 1, G), 8), C), :]
    halo[1] = got[pl.ds(pl.multiple_of(C * lax.rem(me + 1, G), 8), C), :]


def section_kernel(got, other, consts, out, sums, turned):
    row_at, me = lax.axis_index("sec"), lax.axis_index("span")
    half = G // 2 * C
    wide = jnp.concatenate([got[:, 0:C, :].reshape(half, NB), other[:, 0:C, :].reshape(half, NB)], axis=0)
    section = iota((G * C, SECT), 1).astype(F32)
    hot = jnp.where(wide[:, LOWN : LOWN + 1] == section, 1.0, 0.0).astype(BF16)
    full = dot(jnp.concatenate(parts(wide.T), axis=0), hot, ((1,), (0,)))
    sums[...] = full[0:NB] + full[NB : 2 * NB] + full[2 * NB : 3 * NB]
    weights, heats = consts[:, NS : NS + 1], consts[:, NS + 1 : NS + 2]
    block = jnp.concatenate([consts[:, 0:NS]] * 4, axis=1)
    block = jnp.concatenate([block] * 4, axis=0)
    block = jnp.where(iota((NB, NB), 0) // NS == iota((NB, NB), 1) // NS, block, 0.0)
    high, mid, low = parts(block)
    blocks = [jnp.concatenate(pair, axis=1) for pair in ((high, mid), (mid, high), (low, high))]
    first_lane = iota((NS, SECT), 1) == 0

    def rates(tile):
        high, mid, low = parts(tile)
        pairs = (high, mid), (high, mid), (high, low)
        return sum(dot(a, jnp.concatenate(b, axis=0), ((1,), (0,))) for a, b in zip(blocks, pairs))

    def advance(density, moments, bin_at, current, reaction):
        n = density.shape[0]
        weight = jnp.maximum(density, 1.0)
        cond = [m / weight for m in moments]
        eta = ((bin_at + iota((n, SECT), 0)).astype(F32) + 0.5) / NB
        temp = 1.0 + 4.0 * eta * (1.0 - eta) + 0.5 * jnp.tanh(cond[2])
        rate = jnp.exp(2.0 * (1.0 - 1.0 / temp))
        mixing = 0.2 * sigmoid(cond[1])
        carried = 0.3 * sigmoid(cond[0])
        updated, mixes, released = [], [], []
        for r in range(n):
            here = current[r + 1]
            before = jnp.where(first_lane, 0.0, pltpu.roll(here, 1, 1))
            react = reaction[r] * rate[r : r + 1]
            new = (
                here
                + mixing[r : r + 1] * (current[r + 2] + current[r] - 2.0 * here)
                - carried[r : r + 1] * (here - before)
                + 0.2 * react
            )
            updated.append(new)
            mixes.append(jnp.sum(weights * new * new, axis=0, keepdims=True))
            released.append(jnp.sum(heats * react, axis=0, keepdims=True))
        mix = 1.0 + jnp.concatenate(mixes, axis=0) / NS
        rho = 1.0 / (temp * mix)
        temp_c = temp + 0.1 * jnp.concatenate(released, axis=0) - 0.2 * sigmoid(cond[3]) * (temp - 0.5)
        return updated, rho, temp_c

    even = lax.rem(row_at, 2) == 0
    tiles = []
    for t in range(3):
        span = slice(C + G * t, C + G * (t + 1))
        tile = []
        for i in range(G):
            mine, theirs = got[i // 2, span, :], other[i // 2, span, :]
            tile.append(jnp.where(even, mine, theirs) if i % 2 == 0 else jnp.where(even, theirs, mine))
        tiles.append(jnp.concatenate(tile, axis=0).T)
    reacts = [rates(tile) for tile in tiles]
    current = [tiles[b // 4][NS * (b % 4) : NS * (b % 4 + 1)] for b in range(12)]
    reaction = [reacts[b // 4][NS * (b % 4) : NS * (b % 4 + 1)] for b in range(1, 11)]
    first = [sums[LH + 10 * q : LH + 10 * (q + 1), :] for q in range(5)]
    updated, rho, temp0 = advance(first[0], first[1:], 8 * me - 1, current, reaction)
    updated[0] = jnp.where(me == 0, 0.0, updated[0])
    updated[9] = jnp.where(me == G - 1, 0.0, updated[9])
    rho, temp0 = rho[1:9], temp0[1:9]
    count = sums[LC : LC + 8, :]
    moments = [rho * sums[LF + 8 * k : LF + 8 * k + 8, :] for k in range(4)]
    moments[2] = 0.7 * moments[2] + 0.3 * rho * temp0 * count
    reacts = [rates(jnp.concatenate(updated[1 + 4 * t : 5 + 4 * t], axis=0)) for t in range(2)]
    reaction = [reacts[b // 4][NS * (b % 4) : NS * (b % 4 + 1)] for b in range(8)]
    final, rho, temp1 = advance(rho * count, moments, 8 * me, updated, reaction)

    own = got[row_at // 2, 0:C, LOWN : LOWN + 1]
    own = jnp.concatenate([own] * 3 + [jnp.full((NB - 3 * C, 1), -1.0, F32)], axis=0)
    hot = jnp.where(own == iota((NB, SECT), 1).astype(F32), 1.0, 0.0).astype(BF16)
    table = jnp.concatenate([temp0, temp1, rho], axis=0)
    full = dot(jnp.concatenate(parts(table), axis=0), hot, ((1,), (1,)))
    full = full[0:24] + full[24:48] + full[48:72]
    lane = iota((8, NB), 1)
    cells = jnp.where(lane < C, full[0:8], jnp.where(lane < 2 * C, full[8:16], full[16:24]))
    for t in range(2):
        tile = jnp.concatenate(final[4 * t : 4 * t + 4], axis=0)
        turned[t] = jnp.where(row_at < 8, tile[:, 0:NB], tile[:, NB:SECT]).T
    lane = iota((G, NB), 1)
    start = pl.multiple_of(16 * lax.rem(row_at, 8), 16)
    for b in range(8):
        own_sections = turned[b // 4, pl.ds(start, G), :]
        moved = pltpu.roll(own_sections, (96 - 32 * (b % 4)) % NB, 1)
        out[pl.ds(b, G, stride=8), :] = jnp.where(lane >= 96, moved, cells[b : b + 1, :])


def cell_kernel(got, halo, fields, bins, species_to, density_to, fields_to, species_out, density_out, fields_out, left_at):
    leaving = []

    def leave(source, to):
        leaving.append(pltpu.make_async_copy(source, to, left_at.at[len(leaving)]))
        leaving[-1].start()

    table = got[...].reshape(NB, NB).T
    species_out[0] = table[96:128]
    leave(species_out, species_to)
    temp0, temp1, rho = table[0:C], table[C : 2 * C], table[2 * C : 3 * C]

    def look(tab, index):
        return jnp.take_along_axis(tab, index, axis=1)

    def cells(tab):
        return jnp.concatenate([look(tab, bins[:, 0:NB]), look(tab, bins[:, NB:Z])], axis=1)

    density_out[...] = cells(rho)
    leave(density_out, density_to)
    lane = iota((C, Z), 1)
    left, right = halo[0], halo[1]

    def shifted(f, before, after):
        return jnp.where(lane == 0, before, pltpu.roll(f, 1, 1)) + jnp.where(
            lane == Z - 1, after, pltpu.roll(f, Z - 1, 1)
        )

    for k in (2, 0, 1, 3):
        f = fields[k]
        l1, l2 = left[:, LE + 12 + k : LE + 13 + k], left[:, LE + 8 + k : LE + 9 + k]
        r1, r2 = right[:, LE + k : LE + 1 + k], right[:, LE + 4 + k : LE + 5 + k]
        new = f + 0.2 * (shifted(f, l1, r1) - 2.0 * f)
        new_l = l1 + 0.2 * (l2 + f[:, 0:1] - 2.0 * l1)
        new_r = r1 + 0.2 * (f[:, Z - 1 : Z] + r2 - 2.0 * r1)
        if k == 2:
            new = new + 0.3 * (cells(temp0) - new)
            at_l = jnp.broadcast_to(left[:, LB1 : LB1 + 1].astype(jnp.int32), (C, NB))
            at_r = jnp.broadcast_to(right[:, LB0 : LB0 + 1].astype(jnp.int32), (C, NB))
            new_l = new_l + 0.3 * (look(temp0, at_l)[:, 0:1] - new_l)
            new_r = new_r + 0.3 * (look(temp0, at_r)[:, 0:1] - new_r)
        new = new + 0.2 * (shifted(new, new_l, new_r) - 2.0 * new)
        if k == 2:
            new = new + 0.3 * (cells(temp1) - new)
        fields_out[k] = new
        leave(fields_out.at[k], fields_to.at[k])
    for copy in leaving:
        copy.wait()


def call(kernel, name, outs, ins, scratch=(), source=pltpu.VMEM, to=pltpu.VMEM, limit=16 << 20):
    return pl.pallas_call(
        kernel,
        name=name,
        out_shape=[jax.ShapeDtypeStruct(s, F32) for s in outs],
        in_specs=[pl.BlockSpec(memory_space=source)] * len(ins),
        out_specs=[pl.BlockSpec(memory_space=to)] * len(outs),
        scratch_shapes=[pltpu.VMEM(s, F32) if isinstance(s, tuple) else s for s in scratch],
        compiler_params=pltpu.CompilerParams(vmem_limit_bytes=limit),
    )(*ins)


def body(density, fields, bins, owner, species, rate_matrix, inv_weight, formation):
    dma = pltpu.SemaphoreType.DMA
    ins = [bins, fields, density, species, owner.reshape(1, C)]
    ins += [rate_matrix, inv_weight.reshape(1, NS), formation.reshape(1, NS)]
    sent, consts = call(
        bin_kernel,
        "bin",
        [(G, C, NB), (NS, NB)],
        ins,
        [pltpu.VMEM(x.shape, x.dtype) for x in ins]
        + [(2, 48 * C, NB), (16 * C, NB), (264, NB), (C, Z), (G, C, NB), (NS, NB), dma((8,)), dma((G + 1,))],
        pl.ANY,
        pl.ANY,
        (64 << 20) - (64 << 10),
    )
    got = lax.all_to_all(sent, "span", 0, 0, tiled=True)
    sent, halo = call(column_kernel, "column", [(G // 2, R2, NB), (2, C, NB)], [got.reshape(G * C, NB)])
    groups = [list(range(core, G, 2)) for core in range(2)]
    got = lax.all_to_all(sent, "sec", 0, 0, axis_index_groups=groups, tiled=True)
    other = lax.ppermute(got, "sec", [(i, i ^ 1) for i in range(G)])
    (sent,) = call(
        section_kernel,
        "section",
        [(NB, NB)],
        [got, other, consts],
        [(NB, SECT), (2, NB, NB)],
    )
    got = lax.all_to_all(sent.reshape(G, 8, NB), "span", 0, 0, tiled=True)
    outs = [(1, NS, NB), (C, Z), (4, C, Z)]
    return call(cell_kernel, "cell", outs, [got, halo, fields, bins], outs + [dma((6,))], to=pl.ANY)


def solution(mesh):
    return jax.shard_map(
        lambda *args: tuple(body(*args)),
        mesh=mesh,
        in_specs=(
            P("sec", "span"),
            P(None, "sec", "span"),
            P("sec", "span"),
            P("sec"),
            P(("sec", "span"), None, None),
            P(),
            P(),
            P(),
        ),
        out_specs=(P(("sec", "span"), None, None), P("sec", "span"), P(None, "sec", "span")),
        check_vma=False,
    )
```

```python
import jax
import jax.numpy as jnp
from jax import lax
from jax.experimental import pallas as pl
from jax.experimental.pallas import tpu as pltpu
from jax.sharding import PartitionSpec as P

F32, BF16 = jnp.float32, jnp.bfloat16
C, Z, NB, NS = 24, 256, 128, 32
G = 16
SECT = 256
LF, LC, LH, LE = 0, 32, 40, 90
LB0, LB1, LOWN = 106, 107, 108
LS = 112
R2 = C + 3 * G


def iota(shape, dim):
    return lax.broadcasted_iota(jnp.int32, shape, dim)


def parts(value):
    high = value.astype(BF16)
    rest = value - high.astype(F32)
    mid = rest.astype(BF16)
    low = (rest - mid.astype(F32)).astype(BF16)
    return high, mid, low


def column_of(row, n):
    return jnp.sum(jnp.where(iota((n, n), 0) == iota((n, n), 1), row, 0.0), axis=1, keepdims=True)


def sigmoid(x):
    return 0.5 * jnp.tanh(0.5 * x) + 0.5


def dot(a, b, dims):
    return lax.dot_general(a, b, (dims, ((), ())), preferred_element_type=F32)


def bin_kernel(*refs):
    ins, (out, shared), held = refs[0:8], refs[8:10], refs[10:18]
    vals, hist, rows, labels, arrived = refs[18:23]
    bins, fields, den, species, owner, rate_matrix, inv_weight, formation = held
    copies = [pltpu.make_async_copy(ins[n], held[n], arrived.at[n]) for n in range(8)]
    for copy in copies:
        copy.start()
    for copy in copies:
        copy.wait()
    lane = iota((NS, NB), 1)
    block = jnp.concatenate([rate_matrix[...], jnp.zeros((NS, NB - NS), F32)], axis=1)
    block = jnp.where(lane == NS, column_of(inv_weight[...], NS), block)
    shared[...] = jnp.where(lane == NS + 1, column_of(formation[...], NS), block)
    lane = iota((C, Z), 1)
    d = den[...]

    def keep(q, value):
        high, mid, low = parts(value)
        for p, part in enumerate((high, mid, low)):
            at = C * (16 * p + q)
            part = part.astype(F32)
            vals[0, at : at + C, :] = part[:, 0:NB]
            vals[1, at : at + C, :] = part[:, NB:Z]

    keep(0, d)
    keep(5, jnp.ones((C, Z), F32))
    for k in range(4):
        f = fields[k]
        before = jnp.where(lane == 0, 0.0, pltpu.roll(f, 1, 1))
        after = jnp.where(lane == Z - 1, 0.0, pltpu.roll(f, Z - 1, 1))
        keep(1 + k, d * f)
        keep(6 + k, f + 0.2 * (before + after - 2.0 * f))
    for p in range(3):
        at = C * (16 * p + 10)
        for h in range(2):
            vals[h, at : at + 6 * C, :] = jnp.zeros((6 * C, NB), F32)
    labels[...] = bins[...].astype(F32)
    which = iota((NB, Z), 0).astype(F32).astype(BF16).reshape(8, 16, Z)
    one, zero = jnp.ones((8, 16, Z), BF16), jnp.zeros((8, 16, Z), BF16)
    for c in range(C):
        label = jnp.broadcast_to(labels[c : c + 1, :], (16, Z)).astype(BF16)
        hot = jnp.where(which == label[None], one, zero).reshape(NB, Z)
        cells = [vals[h, pl.ds(c, 48, stride=C), :] for h in range(2)]
        full = dot(jnp.concatenate(cells, axis=1).astype(BF16), hot, ((1,), (1,)))
        hist[16 * c : 16 * c + 16, :] = full[0:16] + full[16:32] + full[32:48]
    lane = iota((C, NB), 1)
    edge = jnp.zeros((C, NB), F32)
    for k in range(4):
        first, last = fields[k, :, 0:NB], fields[k, :, Z - NB : Z]
        for e, (tile, at) in enumerate(((first, 0), (first, 1), (last, NB - 2), (last, NB - 1))):
            to = LE + 4 * k + e
            edge = jnp.where(lane == to, pltpu.roll(tile, (to - at) % NB, 1), edge)
    first, last = labels[:, 0:NB], labels[:, Z - NB : Z]
    edge = jnp.where(lane == LB0, pltpu.roll(first, LB0, 1), edge)
    edge = jnp.where(lane == LB1, pltpu.roll(last, (LB1 + 1) % NB, 1), edge)
    edge = jnp.where(lane == LOWN, column_of(owner[...].astype(F32), C), edge)
    sums = [hist[pl.ds(q, C, stride=16), :] for q in range(10)]
    turned = jnp.concatenate([species[0], jnp.zeros((NB - NS, NB), F32)], axis=0).T
    rows[0:8, :] = jnp.zeros((8, NB), F32)
    rows[256:264, :] = jnp.zeros((8, NB), F32)
    rows[pl.ds(4, NB, stride=2), :] = pltpu.roll(turned, LS, 1)
    rows[pl.ds(5, NB, stride=2), :] = pltpu.roll(turned, LS - 16, 1)
    layout = [(LF + 8 * k, 0, 6 + k) for k in range(4)] + [(LC, 0, 5)] + [(LH + 10 * q, -1, q) for q in range(5)]
    turned = [pltpu.roll(sums[q], (start - at) % NB, 1) if start != at else sums[q] for start, at, q in layout]
    for dest in range(G):
        place = lane if dest == 0 else (lane - 8 * dest) & (NB - 1)
        acc = turned[0]
        for n in range(1, 10):
            acc = jnp.where(place >= layout[n][0], turned[n], acc)
        if dest:
            acc = pltpu.roll(acc, NB - 8 * dest, 1)
        acc = jnp.where(lane >= LE, edge, acc)
        acc = jnp.where(lane >= LS, rows[16 * dest : 16 * dest + C, :], acc)
        out[dest] = acc


def column_kernel(got, out, halo):
    me = lax.axis_index("span")
    lane = iota((C, NB), 1)
    total = got[0:C, :]
    for j in range(1, G):
        total = total + got[C * j : C * (j + 1), :]
    source, to = iota((NB, 2 * NB), 0), iota((NB, 2 * NB), 1)
    pick = jnp.where(
        to < 32,
        LE + 3 + 4 * (to // 8),
        jnp.where(
            to < 64,
            LE + 4 * ((to - 32) // 8),
            jnp.where((to >= 128) & (to < 160), LB0, jnp.where((to >= 160) & (to < 192), LB1, -1)),
        ),
    )
    spread = jnp.where(source == pick, 1.0, 0.0).astype(BF16)
    high, mid, low = parts(got[...])
    moved = dot(high, spread, ((1,), (0,))) + dot(mid, spread, ((1,), (0,))) + dot(low, spread, ((1,), (0,)))
    bin_here = (8 * me + lane % 8).astype(F32)
    part = [moved[C * j : C * (j + 1), 0:NB] for j in range(G)]
    fix = jnp.zeros((C, NB), F32)
    for j in range(G):
        beside = jnp.where(lane < 32, part[(j - 1) % G], part[(j + 1) % G])
        fix = fix + jnp.where(moved[C * j : C * (j + 1), NB : 2 * NB] == bin_here, beside, 0.0)
    fix = fix + pltpu.roll(fix, NB - 32, 1)
    total = total + jnp.where(lane < 32, 0.2 * fix, 0.0)
    total = jnp.where(lane >= LE, got[0:C, :], total)
    lane = iota((G, NB), 1)
    tiles = []
    for t in range(3):
        tile = jnp.zeros((G, NB), F32)
        for p in range(8):
            moved = pltpu.roll(got[pl.ds(8 * t + p, G, stride=C), :], (16 * p - LS) % NB, 1)
            tile = jnp.where((lane >= 16 * p) & (lane < 16 * p + 16), moved, tile)
        tiles.append(tile)
    for i in range(G // 2):
        out[i, 0:C, :] = total
        for t in range(3):
            out[i, C + G * t : C + G * (t + 1), :] = tiles[t]
    lane = iota((C, NB), 1)
    left = got[pl.ds(pl.multiple_of(C * lax.rem(me + G - 1, G), 8), C), :]
    right = got[pl.ds(pl.multiple_of(C * lax.rem(me + 1, G), 8), C), :]
    for k in range(4):
        first, last = pltpu.roll(right, NB - LE - 4 * k, 1), pltpu.roll(left, NB - LE - 4 * k - 4, 1)
        halo[k] = jnp.where(lane < 2, first, jnp.where(lane >= NB - 2, last, 0.0))
    first, last = pltpu.roll(right, NB - LB0, 1), pltpu.roll(left, NB - 1 - LB1, 1)
    halo[4] = jnp.where(lane == 0, first, jnp.where(lane == NB - 1, last, 0.0))


def section_kernel(got, other, consts, out, sums, turned):
    row_at, me = lax.axis_index("sec"), lax.axis_index("span")
    half = G // 2 * C
    wide = jnp.concatenate([got[:, 0:C, :].reshape(half, NB), other[:, 0:C, :].reshape(half, NB)], axis=0)
    section = iota((G * C, SECT), 1).astype(F32)
    hot = jnp.where(wide[:, LOWN : LOWN + 1] == section, 1.0, 0.0).astype(BF16)
    full = dot(jnp.concatenate(parts(wide.T), axis=0), hot, ((1,), (0,)))
    sums[...] = full[0:NB] + full[NB : 2 * NB] + full[2 * NB : 3 * NB]
    weights, heats = consts[:, NS : NS + 1], consts[:, NS + 1 : NS + 2]
    block = jnp.concatenate([consts[:, 0:NS]] * 4, axis=1)
    block = jnp.concatenate([block] * 4, axis=0)
    released = jnp.sum(heats * consts[:, 0:NS], axis=0, keepdims=True)
    block = jnp.concatenate([block, jnp.concatenate([jnp.broadcast_to(released, (8, NS))] * 4, axis=1)], axis=0)
    row = iota((NB + 8, NB), 0)
    block = jnp.where(jnp.where(row < NB, row // NS, row - NB) == iota((NB + 8, NB), 1) // NS, block, 0.0)
    high, mid, low = parts(block)
    blocks = [jnp.concatenate(pair, axis=1) for pair in ((high, mid), (mid, high), (low, high))]
    not_first = iota((1, SECT), 1) > 0

    def rates(tile):
        high, mid, low = parts(tile)
        pairs = (high, mid), (high, mid), (high, low)
        return sum(dot(a, jnp.concatenate(b, axis=0), ((1,), (0,))) for a, b in zip(blocks, pairs))

    def advance(density, moments, bin_at, current, reaction, released):
        n = density.shape[0]
        weight = jnp.maximum(density, 1.0)
        cond = [m / weight for m in moments]
        eta = ((bin_at + iota((n, SECT), 0)).astype(F32) + 0.5) / NB
        temp = 1.0 + 4.0 * eta * (1.0 - eta) + 0.5 * jnp.tanh(cond[2])
        rate = jnp.exp(2.0 * (1.0 - 1.0 / temp))
        mixing = 0.2 * sigmoid(cond[1])
        carried = 0.3 * sigmoid(cond[0])
        keep = 1.0 - 2.0 * mixing - carried
        follow = jnp.where(not_first, carried, 0.0)
        grow = 0.2 * rate
        updated, mixes = [], []
        for r in range(n):
            here, row = current[r + 1], slice(r, r + 1)
            new = (
                keep[row] * here
                + mixing[row] * (current[r + 2] + current[r])
                + follow[row] * pltpu.roll(here, 1, 1)
                + grow[row] * reaction[r]
            )
            updated.append(new)
            mixes.append(jnp.sum(weights * new * new, axis=0, keepdims=True))
        mix = 1.0 + jnp.concatenate(mixes, axis=0) / NS
        rho = 1.0 / (temp * mix)
        temp_c = temp + 0.1 * rate * released - 0.2 * sigmoid(cond[3]) * (temp - 0.5)
        return updated, rho, temp_c

    even = lax.rem(row_at, 2) == 0
    tiles = []
    for t in range(3):
        span = slice(C + G * t, C + G * (t + 1))
        tile = []
        for i in range(G):
            mine, theirs = got[i // 2, span, :], other[i // 2, span, :]
            tile.append(jnp.where(even, mine, theirs) if i % 2 == 0 else jnp.where(even, theirs, mine))
        tiles.append(jnp.concatenate(tile, axis=0).T)
    reacts = [rates(tile) for tile in tiles]
    current = [tiles[b // 4][NS * (b % 4) : NS * (b % 4 + 1)] for b in range(12)]
    reaction = [reacts[b // 4][NS * (b % 4) : NS * (b % 4 + 1)] for b in range(1, 11)]
    first = [sums[LH + 10 * q : LH + 10 * (q + 1), :] for q in range(5)]
    released = jnp.concatenate([tile[NB : NB + 4] for tile in reacts], axis=0)[1:11]
    updated, rho, temp0 = advance(first[0], first[1:], 8 * me - 1, current, reaction, released)
    updated[0] = jnp.where(me == 0, 0.0, updated[0])
    updated[9] = jnp.where(me == G - 1, 0.0, updated[9])
    rho, temp0 = rho[1:9], temp0[1:9]
    count = sums[LC : LC + 8, :]
    moments = [rho * sums[LF + 8 * k : LF + 8 * k + 8, :] for k in range(4)]
    moments[2] = 0.7 * moments[2] + 0.3 * rho * temp0 * count
    reacts = [rates(jnp.concatenate(updated[1 + 4 * t : 5 + 4 * t], axis=0)) for t in range(2)]
    reaction = [reacts[b // 4][NS * (b % 4) : NS * (b % 4 + 1)] for b in range(8)]
    released = jnp.concatenate([tile[NB : NB + 4] for tile in reacts], axis=0)
    final, rho, temp1 = advance(rho * count, moments, 8 * me, updated, reaction, released)

    own = got[row_at // 2, 0:C, LOWN : LOWN + 1]
    own = jnp.concatenate([own] * 3 + [jnp.full((NB - 3 * C, 1), -1.0, F32)], axis=0)
    hot = jnp.where(own == iota((NB, SECT), 1).astype(F32), 1.0, 0.0).astype(BF16)
    table = jnp.concatenate([temp0, temp1, rho], axis=0)
    full = dot(jnp.concatenate(parts(table), axis=0), hot, ((1,), (1,)))
    full = full[0:24] + full[24:48] + full[48:72]
    lane = iota((8, NB), 1)
    cells = jnp.where(lane < C, full[0:8], jnp.where(lane < 2 * C, full[8:16], full[16:24]))
    for t in range(2):
        tile = jnp.concatenate(final[4 * t : 4 * t + 4], axis=0)
        turned[t] = jnp.where(row_at < 8, tile[:, 0:NB], tile[:, NB:SECT]).T
    lane = iota((G, NB), 1)
    start = pl.multiple_of(16 * lax.rem(row_at, 8), 16)
    for b in range(8):
        own_sections = turned[b // 4, pl.ds(start, G), :]
        moved = pltpu.roll(own_sections, (96 - 32 * (b % 4)) % NB, 1)
        out[pl.ds(b, G, stride=8), :] = jnp.where(lane >= 96, moved, cells[b : b + 1, :])


def cell_kernel(got, halo, fields, bins, species_to, density_to, fields_to, species_out, density_out, fields_out, left_at):
    leaving = []

    def leave(source, to):
        leaving.append(pltpu.make_async_copy(source, to, left_at.at[len(leaving)]))
        leaving[-1].start()

    table = got[...].reshape(NB, NB).T
    species_out[0] = table[96:128]
    leave(species_out, species_to)
    temp0, temp1, rho = table[0:C], table[C : 2 * C], table[2 * C : 3 * C]

    def look(tab, index):
        return jnp.take_along_axis(tab, index, axis=1)

    index = [bins[:, 0:NB], bins[:, NB:Z], halo[4].astype(jnp.int32)]
    first, last = iota((C, NB), 1) == 0, iota((C, NB), 1) == NB - 1

    def diffused(tiles):
        up, down = [pltpu.roll(t, 1, 1) for t in tiles], [pltpu.roll(t, NB - 1, 1) for t in tiles]
        return [
            t + 0.2 * (jnp.where(first, up[n - 1], up[n]) + jnp.where(last, down[(n + 1) % 3], down[n]) - 2.0 * t)
            for n, t in enumerate(tiles)
        ]

    def relaxed(tiles, tab):
        return [t + 0.3 * (look(tab, i) - t) for t, i in zip(tiles, index)]

    for h in range(2):
        density_out[:, NB * h : NB * (h + 1)] = look(rho, index[h])
    leave(density_out, density_to)
    for k in (2, 0, 1, 3):
        tiles = diffused([fields[k, :, 0:NB], fields[k, :, NB:Z], halo[k]])
        if k == 2:
            tiles = relaxed(tiles, temp0)
        tiles = diffused(tiles)
        if k == 2:
            tiles = relaxed(tiles, temp1)
        for h in range(2):
            fields_out[k, :, NB * h : NB * (h + 1)] = tiles[h]
        leave(fields_out.at[k], fields_to.at[k])
    for copy in leaving:
        copy.wait()


def call(kernel, name, outs, ins, scratch=(), source=pltpu.VMEM, to=pltpu.VMEM):
    return pl.pallas_call(
        kernel,
        name=name,
        out_shape=[jax.ShapeDtypeStruct(s, F32) for s in outs],
        in_specs=[pl.BlockSpec(memory_space=source)] * len(ins),
        out_specs=[pl.BlockSpec(memory_space=to)] * len(outs),
        scratch_shapes=[pltpu.VMEM(s, F32) if isinstance(s, tuple) else s for s in scratch],
        compiler_params=pltpu.CompilerParams(vmem_limit_bytes=16 << 20),
    )(*ins)


def body(density, fields, bins, owner, species, rate_matrix, inv_weight, formation):
    dma = pltpu.SemaphoreType.DMA
    ins = [bins, fields, density, species, owner.reshape(1, C)]
    ins += [rate_matrix, inv_weight.reshape(1, NS), formation.reshape(1, NS)]
    sent, consts = call(
        bin_kernel,
        "bin",
        [(G, C, NB), (NS, NB)],
        [pltpu.with_memory_space_constraint(x, pltpu.HBM) for x in ins],
        [pltpu.VMEM(x.shape, x.dtype) for x in ins]
        + [(2, 48 * C, NB), (16 * C, NB), (264, NB), (C, Z), dma((8,))],
        pltpu.HBM,
    )
    got = lax.all_to_all(sent, "span", 0, 0, tiled=True)
    sent, halo = call(column_kernel, "column", [(G // 2, R2, NB), (5, C, NB)], [got.reshape(G * C, NB)])
    groups = [list(range(core, G, 2)) for core in range(2)]
    got = lax.all_to_all(sent, "sec", 0, 0, axis_index_groups=groups, tiled=True)
    other = lax.ppermute(got, "sec", [(i, i ^ 1) for i in range(G)])
    (sent,) = call(
        section_kernel,
        "section",
        [(NB, NB)],
        [got, other, consts],
        [(NB, SECT), (2, NB, NB)],
    )
    got = lax.all_to_all(sent.reshape(G, 8, NB), "span", 0, 0, tiled=True)
    outs = [(1, NS, NB), (C, Z), (4, C, Z)]
    return call(cell_kernel, "cell", outs, [got, halo, fields, bins], outs + [dma((6,))], to=pl.ANY)


def solution(mesh):
    return jax.shard_map(
        lambda *args: tuple(body(*args)),
        mesh=mesh,
        in_specs=(
            P("sec", "span"),
            P(None, "sec", "span"),
            P("sec", "span"),
            P("sec"),
            P(("sec", "span"), None, None),
            P(),
            P(),
            P(),
        ),
        out_specs=(P(("sec", "span"), None, None), P("sec", "span"), P(None, "sec", "span")),
        check_vma=False,
    )
```

```python
import jax
import jax.numpy as jnp
from jax import lax
from jax.experimental import pallas as pl
from jax.experimental.pallas import tpu as pltpu
from jax.sharding import PartitionSpec as P

F32, BF16 = jnp.float32, jnp.bfloat16
C, Z, NB, NS = 24, 256, 128, 32
G = 16
SECT = 256
LF, LC, LH, LE = 0, 32, 40, 90
LB0, LB1, LOWN = 106, 107, 108
LS = 112
R2 = C + 3 * G


def iota(shape, dim):
    return lax.broadcasted_iota(jnp.int32, shape, dim)


def parts(value):
    high = value.astype(BF16)
    rest = value - high.astype(F32)
    mid = rest.astype(BF16)
    low = (rest - mid.astype(F32)).astype(BF16)
    return high, mid, low


def column_of(row, n):
    return jnp.sum(jnp.where(iota((n, n), 0) == iota((n, n), 1), row, 0.0), axis=1, keepdims=True)


def sigmoid(x):
    return 0.5 * jnp.tanh(0.5 * x) + 0.5


def dot(a, b, dims):
    return lax.dot_general(a, b, (dims, ((), ())), preferred_element_type=F32)


def bin_kernel(*refs):
    ins, (out, shared), held = refs[0:8], refs[8:10], refs[10:18]
    vals, hist, rows, labels, arrived = refs[18:23]
    bins, den, fields, owner, species, rate_matrix, inv_weight, formation = held
    copies = [pltpu.make_async_copy(ins[n], held[n], arrived.at[n]) for n in range(8)]
    for copy in copies:
        copy.start()
    for copy in copies:
        copy.wait()
    lane = iota((NS, NB), 1)
    block = jnp.concatenate([rate_matrix[...], jnp.zeros((NS, NB - NS), F32)], axis=1)
    block = jnp.where(lane == NS, column_of(inv_weight[...], NS), block)
    shared[...] = jnp.where(lane == NS + 1, column_of(formation[...], NS), block)
    lane = iota((C, Z), 1)
    d = den[...]

    def keep(q, value):
        high, mid, low = parts(value)
        for p, part in enumerate((high, mid, low)):
            at = C * (16 * p + q)
            part = part.astype(F32)
            vals[0, at : at + C, :] = part[:, 0:NB]
            vals[1, at : at + C, :] = part[:, NB:Z]

    keep(0, d)
    keep(5, jnp.ones((C, Z), F32))
    for k in range(4):
        f = fields[k]
        before = jnp.where(lane == 0, 0.0, pltpu.roll(f, 1, 1))
        after = jnp.where(lane == Z - 1, 0.0, pltpu.roll(f, Z - 1, 1))
        keep(1 + k, d * f)
        keep(6 + k, f + 0.2 * (before + after - 2.0 * f))
    for p in range(3):
        at = C * (16 * p + 10)
        for h in range(2):
            vals[h, at : at + 6 * C, :] = jnp.zeros((6 * C, NB), F32)
    labels[...] = bins[...].astype(F32)
    which = iota((NB, Z), 0).astype(F32).astype(BF16).reshape(8, 16, Z)
    one, zero = jnp.ones((8, 16, Z), BF16), jnp.zeros((8, 16, Z), BF16)
    for c in range(C):
        label = jnp.broadcast_to(labels[c : c + 1, :], (16, Z)).astype(BF16)
        hot = jnp.where(which == label[None], one, zero).reshape(NB, Z)
        cells = [vals[h, pl.ds(c, 48, stride=C), :] for h in range(2)]
        full = dot(jnp.concatenate(cells, axis=1).astype(BF16), hot, ((1,), (1,)))
        hist[16 * c : 16 * c + 16, :] = full[0:16] + full[16:32] + full[32:48]
    lane = iota((C, NB), 1)
    edge = jnp.zeros((C, NB), F32)
    for k in range(4):
        first, last = fields[k, :, 0:NB], fields[k, :, Z - NB : Z]
        for e, (tile, at) in enumerate(((first, 0), (first, 1), (last, NB - 2), (last, NB - 1))):
            to = LE + 4 * k + e
            edge = jnp.where(lane == to, pltpu.roll(tile, (to - at) % NB, 1), edge)
    first, last = labels[:, 0:NB], labels[:, Z - NB : Z]
    edge = jnp.where(lane == LB0, pltpu.roll(first, LB0, 1), edge)
    edge = jnp.where(lane == LB1, pltpu.roll(last, (LB1 + 1) % NB, 1), edge)
    edge = jnp.where(lane == LOWN, column_of(owner[...].astype(F32), C), edge)
    sums = [hist[pl.ds(q, C, stride=16), :] for q in range(10)]
    turned = jnp.concatenate([species[0], jnp.zeros((NB - NS, NB), F32)], axis=0).T
    rows[0:8, :] = jnp.zeros((8, NB), F32)
    rows[256:264, :] = jnp.zeros((8, NB), F32)
    rows[pl.ds(4, NB, stride=2), :] = pltpu.roll(turned, LS, 1)
    rows[pl.ds(5, NB, stride=2), :] = pltpu.roll(turned, LS - 16, 1)
    layout = [(LF + 8 * k, 0, 6 + k) for k in range(4)] + [(LC, 0, 5)] + [(LH + 10 * q, -1, q) for q in range(5)]
    turned = [pltpu.roll(sums[q], (start - at) % NB, 1) if start != at else sums[q] for start, at, q in layout]
    for dest in range(G):
        place = lane if dest == 0 else (lane - 8 * dest) & (NB - 1)
        acc = turned[0]
        for n in range(1, 10):
            acc = jnp.where(place >= layout[n][0], turned[n], acc)
        if dest:
            acc = pltpu.roll(acc, NB - 8 * dest, 1)
        acc = jnp.where(lane >= LE, edge, acc)
        acc = jnp.where(lane >= LS, rows[16 * dest : 16 * dest + C, :], acc)
        out[dest] = acc


def column_kernel(got, out, halo):
    me = lax.axis_index("span")
    lane = iota((C, NB), 1)
    total = got[0:C, :]
    for j in range(1, G):
        total = total + got[C * j : C * (j + 1), :]
    source, to = iota((NB, 2 * NB), 0), iota((NB, 2 * NB), 1)
    pick = jnp.where(
        to < 32,
        LE + 3 + 4 * (to // 8),
        jnp.where(
            to < 64,
            LE + 4 * ((to - 32) // 8),
            jnp.where((to >= 128) & (to < 160), LB0, jnp.where((to >= 160) & (to < 192), LB1, -1)),
        ),
    )
    spread = jnp.where(source == pick, 1.0, 0.0).astype(BF16)
    high, mid, low = parts(got[...])
    moved = dot(high, spread, ((1,), (0,))) + dot(mid, spread, ((1,), (0,))) + dot(low, spread, ((1,), (0,)))
    bin_here = (8 * me + lane % 8).astype(F32)
    part = [moved[C * j : C * (j + 1), 0:NB] for j in range(G)]
    fix = jnp.zeros((C, NB), F32)
    for j in range(G):
        beside = jnp.where(lane < 32, part[(j - 1) % G], part[(j + 1) % G])
        fix = fix + jnp.where(moved[C * j : C * (j + 1), NB : 2 * NB] == bin_here, beside, 0.0)
    fix = fix + pltpu.roll(fix, NB - 32, 1)
    total = total + jnp.where(lane < 32, 0.2 * fix, 0.0)
    total = jnp.where(lane >= LE, got[0:C, :], total)
    lane = iota((G, NB), 1)
    tiles = []
    for t in range(3):
        tile = jnp.zeros((G, NB), F32)
        for p in range(8):
            moved = pltpu.roll(got[pl.ds(8 * t + p, G, stride=C), :], (16 * p - LS) % NB, 1)
            tile = jnp.where((lane >= 16 * p) & (lane < 16 * p + 16), moved, tile)
        tiles.append(tile)
    for i in range(G // 2):
        out[i, 0:C, :] = total
        for t in range(3):
            out[i, C + G * t : C + G * (t + 1), :] = tiles[t]
    lane = iota((C, NB), 1)
    left = got[pl.ds(pl.multiple_of(C * lax.rem(me + G - 1, G), 8), C), :]
    right = got[pl.ds(pl.multiple_of(C * lax.rem(me + 1, G), 8), C), :]
    for k in range(4):
        first, last = pltpu.roll(right, NB - LE - 4 * k, 1), pltpu.roll(left, NB - LE - 4 * k - 4, 1)
        halo[k] = jnp.where(lane < 2, first, jnp.where(lane >= NB - 2, last, 0.0))
    first, last = pltpu.roll(right, NB - LB0, 1), pltpu.roll(left, NB - 1 - LB1, 1)
    halo[4] = jnp.where(lane == 0, first, jnp.where(lane == NB - 1, last, 0.0))


def section_lane(owner, core):
    owner = owner.astype(jnp.int32)
    return (owner >> 5) * 16 + (owner & 15) + jnp.where(((owner >> 4) & 1) == core, 0, NB)


def rates(blocks, tile):
    high = tile.astype(BF16)
    mid = (tile - high.astype(F32)).astype(BF16)
    pair = dot(blocks[:, 0 : 2 * NB], jnp.concatenate([high, high], axis=0), ((1,), (0,)))
    return (pair + dot(blocks[:, 0:NB], mid, ((1,), (0,))))[0 : NB + 8]


def half_sums(got, core, blocks, species, reacts):
    wide = got[:, 0:C, :].reshape(G // 2 * C, NB)
    lane = section_lane(wide[:, LOWN : LOWN + 1], core)
    hot = jnp.where(lane == iota((G // 2 * C, SECT), 1), 1.0, 0.0).astype(BF16)
    full = dot(jnp.concatenate(parts(wide.T), axis=0), hot, ((1,), (0,)))
    for t in range(3):
        tile = got[:, C + G * t : C + G * (t + 1), :].reshape(NB, NB).T
        species[t] = tile
        reacts[t] = rates(blocks, tile)
    return full[0:NB] + full[NB : 2 * NB] + full[2 * NB : 3 * NB]


def diffused(tiles):
    first, last = iota((C, NB), 1) == 0, iota((C, NB), 1) == NB - 1
    up, down = [pltpu.roll(t, 1, 1) for t in tiles], [pltpu.roll(t, NB - 1, 1) for t in tiles]
    return [
        t + 0.2 * (jnp.where(first, up[n - 1], up[n]) + jnp.where(last, down[(n + 1) % 3], down[n]) - 2.0 * t)
        for n, t in enumerate(tiles)
    ]


def own_kernel(got, consts, halo, fields, sums, species, reacts, blocks, once, early):
    for n, k in enumerate((0, 1, 3, 2)):
        tiles = diffused([fields[k, :, 0:NB], fields[k, :, NB:Z], halo[k]])
        if k == 2:
            for h in range(3):
                once[h] = tiles[h]
            continue
        tiles = diffused(tiles)
        for h in range(2):
            early[n, :, NB * h : NB * (h + 1)] = tiles[h]
    block = jnp.concatenate([consts[:, 0:NS]] * 4, axis=1)
    block = jnp.concatenate([block] * 4, axis=0)
    released = jnp.sum(consts[:, NS + 1 : NS + 2] * consts[:, 0:NS], axis=0, keepdims=True)
    block = jnp.concatenate([block, jnp.concatenate([jnp.broadcast_to(released, (8, NS))] * 4, axis=1)], axis=0)
    row = iota((NB + 8, NB), 0)
    block = jnp.where(jnp.where(row < NB, row // NS, row - NB) == iota((NB + 8, NB), 1) // NS, block, 0.0)
    high, mid, _ = parts(block)
    blocks[0 : NB + 8, 0:NB] = high
    blocks[0 : NB + 8, NB : 2 * NB] = mid
    blocks[NB + 8 : NB + 16, :] = jnp.zeros((8, 2 * NB), BF16)
    core = lax.rem(lax.axis_index("sec"), 2)
    sums[...] = half_sums(got, core, blocks, species, reacts)


def section_kernel(got, other, consts, own_sums, own_species, own_reacts, blocks, out, sums, species, reacts, mid, turned):
    row_at, me = lax.axis_index("sec"), lax.axis_index("span")
    core = lax.rem(row_at, 2)
    sums[...] = own_sums[...] + half_sums(other, core, blocks, species, reacts)
    weights = consts[:, NS : NS + 1]
    lane = iota((NS, NB), 1)
    starts = (lane & 15) == 0
    section_0 = iota((1, SECT), 1) == NB * core
    near, far = jnp.where(core == 0, 1, NB - 15), jnp.where(core == 0, NB - 15, 1)

    def advance(density, moments, bin_at, current, reaction, released):
        n = density.shape[0]
        weight = jnp.maximum(density, 1.0)
        cond = [m / weight for m in moments]
        eta = ((bin_at + iota((n, SECT), 0)).astype(F32) + 0.5) / NB
        temp = 1.0 + 4.0 * eta * (1.0 - eta) + 0.5 * jnp.tanh(cond[2])
        rate = jnp.exp(2.0 * (1.0 - 1.0 / temp))
        mixing = 0.2 * sigmoid(cond[1])
        carried = 0.3 * sigmoid(cond[0])
        keep = 1.0 - 2.0 * mixing - carried
        follow = jnp.where(section_0, 0.0, carried)
        grow = 0.2 * rate
        updated, mixes = [], []
        for r in range(n):
            here = current(r + 1)
            above, below, react, row = current(r + 2), current(r), reaction(r), slice(r, r + 1)
            before = (
                jnp.where(starts, pltpu.roll(here[1], near, 1), pltpu.roll(here[0], 1, 1)),
                jnp.where(starts, pltpu.roll(here[0], far, 1), pltpu.roll(here[1], 1, 1)),
            )
            new = []
            for h in range(2):
                half = slice(NB * h, NB * (h + 1))
                new.append(
                    keep[row, half] * here[h]
                    + mixing[row, half] * (above[h] + below[h])
                    + follow[row, half] * before[h]
                    + grow[row, half] * react[h]
                )
            updated.append(new)
            mixes.append(
                jnp.concatenate([jnp.sum(weights * x * x, axis=0, keepdims=True) for x in new], axis=1)
            )
        mix = 1.0 + jnp.concatenate(mixes, axis=0) / NS
        rho = 1.0 / (temp * mix)
        temp_c = temp + 0.1 * rate * released - 0.2 * sigmoid(cond[3]) * (temp - 0.5)
        return updated, rho, temp_c

    def current(b):
        rows = slice(NS * (b % 4), NS * (b % 4 + 1))
        return own_species[b // 4, rows, :], species[b // 4, rows, :]

    def reaction(r):
        rows = slice(NS * ((r + 1) % 4), NS * ((r + 1) % 4 + 1))
        return own_reacts[(r + 1) // 4, rows, :], reacts[(r + 1) // 4, rows, :]

    released = [[x[t, NB : NB + 4, :] for t in range(3)] for x in (own_reacts, reacts)]
    released = jnp.concatenate([jnp.concatenate(x, axis=0)[1:11] for x in released], axis=1)
    first = [sums[LH + 10 * q : LH + 10 * (q + 1), :] for q in range(5)]
    updated, rho, temp0 = advance(first[0], first[1:], 8 * me - 1, current, reaction, released)
    updated[0] = [jnp.where(me == 0, 0.0, x) for x in updated[0]]
    updated[9] = [jnp.where(me == G - 1, 0.0, x) for x in updated[9]]
    for r in range(10):
        for h in range(2):
            mid[NS * r : NS * (r + 1), NB * h : NB * (h + 1)] = updated[r][h]
    rho, temp0 = rho[1:9], temp0[1:9]
    count = sums[LC : LC + 8, :]
    moments = [rho * sums[LF + 8 * k : LF + 8 * k + 8, :] for k in range(4)]
    moments[2] = 0.7 * moments[2] + 0.3 * rho * temp0 * count
    later = [rates(blocks, mid[NS + NB * t : NS + NB * (t + 1), :]) for t in range(2)]

    def current(b):
        return [mid[NS * b : NS * (b + 1), NB * h : NB * (h + 1)] for h in range(2)]

    def reaction(r):
        return [later[r // 4][NS * (r % 4) : NS * (r % 4 + 1), NB * h : NB * (h + 1)] for h in range(2)]

    released = jnp.concatenate([x[NB : NB + 4] for x in later], axis=0)
    final, rho, temp1 = advance(rho * count, moments, 8 * me, current, reaction, released)

    own = section_lane(got[row_at // 2, 0:C, LOWN : LOWN + 1], core)
    own = jnp.concatenate([own] * 3 + [jnp.full((NB - 3 * C, 1), -1, jnp.int32)], axis=0)
    hot = jnp.where(own == iota((NB, SECT), 1), 1.0, 0.0).astype(BF16)
    table = jnp.concatenate([temp0, temp1, rho], axis=0)
    full = dot(jnp.concatenate(parts(table), axis=0), hot, ((1,), (1,)))
    full = full[0:24] + full[24:48] + full[48:72]
    lane = iota((8, NB), 1)
    cells = jnp.where(lane < C, full[0:8], jnp.where(lane < 2 * C, full[8:16], full[16:24]))
    for t in range(2):
        turned[t] = jnp.concatenate([x[0] for x in final[4 * t : 4 * t + 4]], axis=0).T
    lane = iota((G, NB), 1)
    start = pl.multiple_of(16 * (row_at // 2), 16)
    for b in range(8):
        own_sections = turned[b // 4, pl.ds(start, G), :]
        moved = pltpu.roll(own_sections, (96 - 32 * (b % 4)) % NB, 1)
        out[pl.ds(b, G, stride=8), :] = jnp.where(lane >= 96, moved, cells[b : b + 1, :])


def cell_kernel(got, halo, bins, once, early, species_to, density_to, fields_to, species_out, density_out, field, left_at):
    leaving = []

    def leave(source, to):
        leaving.append(pltpu.make_async_copy(source, to, left_at.at[len(leaving)]))
        leaving[-1].start()

    for n, k in enumerate((0, 1, 3)):
        leave(early.at[n], fields_to.at[k])
    table = got[...].reshape(NB, NB).T
    temp0, temp1, rho = table[0:C], table[C : 2 * C], table[2 * C : 3 * C]
    index = [bins[:, 0:NB], bins[:, NB:Z], halo[4].astype(jnp.int32)]

    def look(tab, index):
        return jnp.take_along_axis(tab, index, axis=1)

    def relaxed(tiles, tab):
        return [t + 0.3 * (look(tab, i) - t) for t, i in zip(tiles, index)]

    species_out[0] = table[96:128]
    leave(species_out, species_to)
    for h in range(2):
        density_out[:, NB * h : NB * (h + 1)] = look(rho, index[h])
    leave(density_out, density_to)
    tiles = relaxed(diffused(relaxed([once[h] for h in range(3)], temp0)), temp1)
    for h in range(2):
        field[:, NB * h : NB * (h + 1)] = tiles[h]
    leave(field, fields_to.at[2])
    for copy in leaving:
        copy.wait()


def call(kernel, name, outs, ins, scratch=(), source=pltpu.VMEM):
    outs = [(pltpu.VMEM, jax.ShapeDtypeStruct(s, F32)) if isinstance(s[0], int) else s for s in outs]
    return pl.pallas_call(
        kernel,
        name=name,
        out_shape=[s if space == pltpu.VMEM else space(s.shape, s.dtype) for space, s in outs],
        in_specs=[pl.BlockSpec(memory_space=source)] * len(ins),
        out_specs=[pl.BlockSpec(memory_space=space) for space, _ in outs],
        scratch_shapes=[pltpu.VMEM(s, F32) if isinstance(s, tuple) else s for s in scratch],
        compiler_params=pltpu.CompilerParams(vmem_limit_bytes=16 << 20),
    )(*ins)


def body(density, fields, bins, owner, species, rate_matrix, inv_weight, formation):
    dma = pltpu.SemaphoreType.DMA
    ins = [bins, density, fields, owner.reshape(1, C)]
    ins += [species, rate_matrix, inv_weight.reshape(1, NS), formation.reshape(1, NS)]
    sent, consts = call(
        bin_kernel,
        "bin",
        [(G, C, NB), (NS, NB)],
        [pltpu.with_memory_space_constraint(x, pltpu.HBM) for x in ins],
        [pltpu.VMEM(x.shape, x.dtype) for x in ins]
        + [(2, 48 * C, NB), (16 * C, NB), (264, NB), (C, Z), dma((8,))],
        pltpu.HBM,
    )
    got = lax.all_to_all(sent, "span", 0, 0, tiled=True)
    sent, halo = call(column_kernel, "column", [(G // 2, R2, NB), (5, C, NB)], [got.reshape(G * C, NB)])
    groups = [list(range(core, G, 2)) for core in range(2)]
    got = lax.all_to_all(sent, "sec", 0, 0, axis_index_groups=groups, tiled=True)
    other = lax.ppermute(got, "sec", [(i, i ^ 1) for i in range(G)])
    halves = [(NB, SECT), (3, NB, NB), (3, NB + 8, NB)]
    blocks = (pltpu.VMEM, jax.ShapeDtypeStruct((NB + 16, 2 * NB), BF16))
    far = [(pltpu.HBM, jax.ShapeDtypeStruct(s, F32)) for s in ((1, NS, NB), (C, Z), (4, C, Z))]
    *own, once, early = call(
        own_kernel, "own", halves + [blocks, (3, C, NB), (3, C, Z)], [got, consts, halo, fields]
    )
    scratch = halves + [(10 * NS, SECT), (2, NB, NB)]
    (sent,) = call(section_kernel, "section", [(NB, NB)], [got, other, consts] + own, scratch)
    got = lax.all_to_all(sent.reshape(G, 8, NB), "span", 0, 0, tiled=True)
    scratch = [(1, NS, NB), (C, Z), (C, Z), dma((6,))]
    return call(cell_kernel, "cell", far, [got, halo, bins, once, early], scratch)


def solution(mesh):
    return jax.shard_map(
        lambda *args: tuple(body(*args)),
        mesh=mesh,
        in_specs=(
            P("sec", "span"),
            P(None, "sec", "span"),
            P("sec", "span"),
            P("sec"),
            P(("sec", "span"), None, None),
            P(),
            P(),
            P(),
        ),
        out_specs=(P(("sec", "span"), None, None), P("sec", "span"), P(None, "sec", "span")),
        check_vma=False,
    )
```

```python
import jax
import jax.numpy as jnp
from jax import lax
from jax.experimental import pallas as pl
from jax.experimental.pallas import tpu as pltpu
from jax.sharding import PartitionSpec as P

F32, BF16 = jnp.float32, jnp.bfloat16
C, Z, NB, NS = 24, 256, 128, 32
G = 16
SECT = 256
LF, LC, LH, LE = 0, 32, 40, 90
LB0, LB1, LOWN = 106, 107, 108
LS = 112
R2 = C + 3 * G


def iota(shape, dim):
    return lax.broadcasted_iota(jnp.int32, shape, dim)


def parts(value):
    high = value.astype(BF16)
    rest = value - high.astype(F32)
    mid = rest.astype(BF16)
    low = (rest - mid.astype(F32)).astype(BF16)
    return high, mid, low


def column_of(row, n):
    return jnp.sum(jnp.where(iota((n, n), 0) == iota((n, n), 1), row, 0.0), axis=1, keepdims=True)


def sigmoid(x):
    return 0.5 * jnp.tanh(0.5 * x) + 0.5


def dot(a, b, dims):
    return lax.dot_general(a, b, (dims, ((), ())), preferred_element_type=F32)


def bin_kernel(*refs):
    ins, (out, shared), held = refs[0:8], refs[8:10], refs[10:18]
    vals, hist, rows, labels, arrived = refs[18:23]
    bins, den, fields, owner, species, rate_matrix, inv_weight, formation = held
    moves = [(ins[n], held[n]) for n in (0, 1, 3, 4, 5, 6, 7)]
    moves += [(ins[2].at[k], held[2].at[k]) for k in range(4)]
    copies = [pltpu.make_async_copy(source, to, arrived.at[n]) for n, (source, to) in enumerate(moves)]
    for copy in copies:
        copy.start()

    def keep(q, value):
        high, mid, low = parts(value)
        for p, part in enumerate((high, mid, low)):
            at = C * (16 * p + q)
            part = part.astype(F32)
            vals[0, at : at + C, :] = part[:, 0:NB]
            vals[1, at : at + C, :] = part[:, NB:Z]

    keep(5, jnp.ones((C, Z), F32))
    for p in range(3):
        at = C * (16 * p + 10)
        for h in range(2):
            vals[h, at : at + 6 * C, :] = jnp.zeros((6 * C, NB), F32)
    rows[0:8, :] = jnp.zeros((8, NB), F32)
    rows[256:264, :] = jnp.zeros((8, NB), F32)
    for copy in copies:
        copy.wait()
    lane = iota((NS, NB), 1)
    block = jnp.concatenate([rate_matrix[...], jnp.zeros((NS, NB - NS), F32)], axis=1)
    block = jnp.where(lane == NS, column_of(inv_weight[...], NS), block)
    shared[...] = jnp.where(lane == NS + 1, column_of(formation[...], NS), block)
    lane = iota((C, Z), 1)
    d = den[...]

    keep(0, d)
    for k in range(4):
        f = fields[k]
        before = jnp.where(lane == 0, 0.0, pltpu.roll(f, 1, 1))
        after = jnp.where(lane == Z - 1, 0.0, pltpu.roll(f, Z - 1, 1))
        keep(1 + k, d * f)
        keep(6 + k, f + 0.2 * (before + after - 2.0 * f))
    labels[...] = bins[...].astype(F32)
    which = iota((NB, Z), 0).astype(F32).astype(BF16).reshape(8, 16, Z)
    one, zero = jnp.ones((8, 16, Z), BF16), jnp.zeros((8, 16, Z), BF16)
    for c in range(C):
        label = jnp.broadcast_to(labels[c : c + 1, :], (16, Z)).astype(BF16)
        hot = jnp.where(which == label[None], one, zero).reshape(NB, Z)
        cells = [vals[h, pl.ds(c, 48, stride=C), :] for h in range(2)]
        full = dot(jnp.concatenate(cells, axis=1).astype(BF16), hot, ((1,), (1,)))
        hist[16 * c : 16 * c + 16, :] = full[0:16] + full[16:32] + full[32:48]
    lane = iota((C, NB), 1)
    edge = jnp.zeros((C, NB), F32)
    for k in range(4):
        first, last = fields[k, :, 0:NB], fields[k, :, Z - NB : Z]
        for e, (tile, at) in enumerate(((first, 0), (first, 1), (last, NB - 2), (last, NB - 1))):
            to = LE + 4 * k + e
            edge = jnp.where(lane == to, pltpu.roll(tile, (to - at) % NB, 1), edge)
    first, last = labels[:, 0:NB], labels[:, Z - NB : Z]
    edge = jnp.where(lane == LB0, pltpu.roll(first, LB0, 1), edge)
    edge = jnp.where(lane == LB1, pltpu.roll(last, (LB1 + 1) % NB, 1), edge)
    edge = jnp.where(lane == LOWN, column_of(owner[...].astype(F32), C), edge)
    sums = [hist[pl.ds(q, C, stride=16), :] for q in range(10)]
    turned = jnp.concatenate([species[0], jnp.zeros((NB - NS, NB), F32)], axis=0).T
    rows[pl.ds(4, NB, stride=2), :] = pltpu.roll(turned, LS, 1)
    rows[pl.ds(5, NB, stride=2), :] = pltpu.roll(turned, LS - 16, 1)
    layout = [(LF + 8 * k, 0, 6 + k) for k in range(4)] + [(LC, 0, 5)] + [(LH + 10 * q, -1, q) for q in range(5)]
    turned = [pltpu.roll(sums[q], (start - at) % NB, 1) if start != at else sums[q] for start, at, q in layout]
    for dest in range(G):
        place = lane if dest == 0 else (lane - 8 * dest) & (NB - 1)
        acc = turned[0]
        for n in range(1, 10):
            acc = jnp.where(place >= layout[n][0], turned[n], acc)
        if dest:
            acc = pltpu.roll(acc, NB - 8 * dest, 1)
        acc = jnp.where(lane >= LE, edge, acc)
        acc = jnp.where(lane >= LS, rows[16 * dest : 16 * dest + C, :], acc)
        out[dest] = acc


def column_kernel(got, out, halo):
    me = lax.axis_index("span")
    lane = iota((C, NB), 1)
    total = got[0:C, :]
    for j in range(1, G):
        total = total + got[C * j : C * (j + 1), :]
    source, to = iota((NB, 2 * NB), 0), iota((NB, 2 * NB), 1)
    pick = jnp.where(
        to < 32,
        LE + 3 + 4 * (to // 8),
        jnp.where(
            to < 64,
            LE + 4 * ((to - 32) // 8),
            jnp.where((to >= 128) & (to < 160), LB0, jnp.where((to >= 160) & (to < 192), LB1, -1)),
        ),
    )
    spread = jnp.where(source == pick, 1.0, 0.0).astype(BF16)
    high, mid, low = parts(got[...])
    moved = dot(high, spread, ((1,), (0,))) + dot(mid, spread, ((1,), (0,))) + dot(low, spread, ((1,), (0,)))
    bin_here = (8 * me + lane % 8).astype(F32)
    part = [moved[C * j : C * (j + 1), 0:NB] for j in range(G)]
    fix = jnp.zeros((C, NB), F32)
    for j in range(G):
        beside = jnp.where(lane < 32, part[(j - 1) % G], part[(j + 1) % G])
        fix = fix + jnp.where(moved[C * j : C * (j + 1), NB : 2 * NB] == bin_here, beside, 0.0)
    fix = fix + pltpu.roll(fix, NB - 32, 1)
    total = total + jnp.where(lane < 32, 0.2 * fix, 0.0)
    total = jnp.where(lane >= LE, got[0:C, :], total)
    lane = iota((G, NB), 1)
    tiles = []
    for t in range(3):
        tile = jnp.zeros((G, NB), F32)
        for p in range(8):
            moved = pltpu.roll(got[pl.ds(8 * t + p, G, stride=C), :], (16 * p - LS) % NB, 1)
            tile = jnp.where((lane >= 16 * p) & (lane < 16 * p + 16), moved, tile)
        tiles.append(tile)
    for i in range(G // 2):
        out[i, 0:C, :] = total
        for t in range(3):
            out[i, C + G * t : C + G * (t + 1), :] = tiles[t]
    lane = iota((C, NB), 1)
    left = got[pl.ds(pl.multiple_of(C * lax.rem(me + G - 1, G), 8), C), :]
    right = got[pl.ds(pl.multiple_of(C * lax.rem(me + 1, G), 8), C), :]
    for k in range(4):
        first, last = pltpu.roll(right, NB - LE - 4 * k, 1), pltpu.roll(left, NB - LE - 4 * k - 4, 1)
        halo[k] = jnp.where(lane < 2, first, jnp.where(lane >= NB - 2, last, 0.0))
    first, last = pltpu.roll(right, NB - LB0, 1), pltpu.roll(left, NB - 1 - LB1, 1)
    halo[4] = jnp.where(lane == 0, first, jnp.where(lane == NB - 1, last, 0.0))


def section_lane(owner, core):
    owner = owner.astype(jnp.int32)
    return (owner >> 5) * 16 + (owner & 15) + jnp.where(((owner >> 4) & 1) == core, 0, NB)


def rates(blocks, tile):
    high = tile.astype(BF16)
    mid = (tile - high.astype(F32)).astype(BF16)
    pair = dot(blocks[:, 0 : 2 * NB], jnp.concatenate([high, high], axis=0), ((1,), (0,)))
    return (pair + dot(blocks[:, 0:NB], mid, ((1,), (0,))))[0 : NB + 8]


def half_sums(got, core, blocks, species, reacts):
    wide = got[:, 0:C, :].reshape(G // 2 * C, NB)
    lane = section_lane(wide[:, LOWN : LOWN + 1], core)
    hot = jnp.where(lane == iota((G // 2 * C, SECT), 1), 1.0, 0.0).astype(BF16)
    full = dot(jnp.concatenate(parts(wide.T), axis=0), hot, ((1,), (0,)))
    for t in range(3):
        tile = got[:, C + G * t : C + G * (t + 1), :].reshape(NB, NB).T
        species[t] = tile
        reacts[t] = rates(blocks, tile)
    return full[0:NB] + full[NB : 2 * NB] + full[2 * NB : 3 * NB]


def diffused(tiles):
    first, last = iota((C, NB), 1) == 0, iota((C, NB), 1) == NB - 1
    up, down = [pltpu.roll(t, 1, 1) for t in tiles], [pltpu.roll(t, NB - 1, 1) for t in tiles]
    return [
        t + 0.2 * (jnp.where(first, up[n - 1], up[n]) + jnp.where(last, down[(n + 1) % 3], down[n]) - 2.0 * t)
        for n, t in enumerate(tiles)
    ]


def own_kernel(got, consts, halo, fields, sums, species, reacts, blocks, once, early):
    for n, k in enumerate((0, 1, 3, 2)):
        tiles = diffused([fields[k, :, 0:NB], fields[k, :, NB:Z], halo[k]])
        if k == 2:
            for h in range(3):
                once[h] = tiles[h]
            continue
        tiles = diffused(tiles)
        for h in range(2):
            early[n, :, NB * h : NB * (h + 1)] = tiles[h]
    block = jnp.concatenate([consts[:, 0:NS]] * 4, axis=1)
    block = jnp.concatenate([block] * 4, axis=0)
    released = jnp.sum(consts[:, NS + 1 : NS + 2] * consts[:, 0:NS], axis=0, keepdims=True)
    block = jnp.concatenate([block, jnp.concatenate([jnp.broadcast_to(released, (8, NS))] * 4, axis=1)], axis=0)
    row = iota((NB + 8, NB), 0)
    block = jnp.where(jnp.where(row < NB, row // NS, row - NB) == iota((NB + 8, NB), 1) // NS, block, 0.0)
    high, mid, _ = parts(block)
    blocks[0 : NB + 8, 0:NB] = high
    blocks[0 : NB + 8, NB : 2 * NB] = mid
    blocks[NB + 8 : NB + 16, :] = jnp.zeros((8, 2 * NB), BF16)
    core = lax.rem(lax.axis_index("sec"), 2)
    sums[...] = half_sums(got, core, blocks, species, reacts)


def section_kernel(got, other, consts, own_sums, own_species, own_reacts, blocks, out, sums, species, reacts, mid, turned, rows_of):
    row_at, me = lax.axis_index("sec"), lax.axis_index("span")
    core = lax.rem(row_at, 2)
    sums[...] = own_sums[...] + half_sums(other, core, blocks, species, reacts)
    weights = consts[:, NS : NS + 1]
    lane = iota((NS, NB), 1)
    starts = (lane & 15) == 0
    section_0 = iota((1, SECT), 1) == NB * core
    near, far = jnp.where(core == 0, 1, NB - 15), jnp.where(core == 0, NB - 15, 1)

    def advance(density, moments, bin_at, current, reaction, released, put):
        n = density.shape[0]
        inner = slice(1, 9) if n == 10 else slice(0, 8)
        weight = jnp.maximum(density, 1.0)
        cond = [m / weight for m in moments]
        eta = ((bin_at + iota((n, SECT), 0)).astype(F32) + 0.5) / NB
        temp = 1.0 + 4.0 * eta * (1.0 - eta) + 0.5 * jnp.tanh(cond[2])
        rate = jnp.exp(2.0 * (1.0 - 1.0 / temp))
        mixing = 0.2 * sigmoid(cond[1])
        carried = 0.3 * sigmoid(cond[0])
        follow = jnp.where(section_0, 0.0, carried)
        for c, coefficient in enumerate((1.0 - 2.0 * mixing - carried, mixing, follow, 0.2 * rate)):
            rows_of[16 * c : 16 * c + n, :] = coefficient
        mixes = []
        for r in range(n):
            here = current(r + 1)
            above, below, react = current(r + 2), current(r), reaction(r)
            before = (
                jnp.where(starts, pltpu.roll(here[1], near, 1), pltpu.roll(here[0], 1, 1)),
                jnp.where(starts, pltpu.roll(here[0], far, 1), pltpu.roll(here[1], 1, 1)),
            )
            new = []
            for h in range(2):
                half = slice(NB * h, NB * (h + 1))
                keep, spread, follow, grow = [rows_of[16 * c + r : 16 * c + r + 1, half] for c in range(4)]
                new.append(keep * here[h] + spread * (above[h] + below[h]) + follow * before[h] + grow * react[h])
            put(r, new)
            if inner.start <= r < inner.stop:
                mixes.append(
                    jnp.concatenate([jnp.sum(weights * x * x, axis=0, keepdims=True) for x in new], axis=1)
                )
        mix = 1.0 + jnp.concatenate(mixes, axis=0) / NS
        temp, rate, loss = temp[inner], rate[inner], cond[3][inner]
        rho = 1.0 / (temp * mix)
        temp_c = temp + 0.1 * rate * released - 0.2 * sigmoid(loss) * (temp - 0.5)
        return rho, temp_c

    def current(b):
        rows = slice(NS * (b % 4), NS * (b % 4 + 1))
        return own_species[b // 4, rows, :], species[b // 4, rows, :]

    def reaction(r):
        rows = slice(NS * ((r + 1) % 4), NS * ((r + 1) % 4 + 1))
        return own_reacts[(r + 1) // 4, rows, :], reacts[(r + 1) // 4, rows, :]

    released = [[x[t, NB : NB + 4, :] for t in range(3)] for x in (own_reacts, reacts)]
    released = jnp.concatenate([jnp.concatenate(x, axis=0)[2:10] for x in released], axis=1)
    first = [sums[LH + 10 * q : LH + 10 * (q + 1), :] for q in range(5)]

    def put(r, new):
        outside = (me == 0) if r == 0 else (me == G - 1) if r == 9 else None
        for h in range(2):
            value = new[h] if outside is None else jnp.where(outside, 0.0, new[h])
            mid[NS * r : NS * (r + 1), NB * h : NB * (h + 1)] = value

    rho, temp0 = advance(first[0], first[1:], 8 * me - 1, current, reaction, released, put)
    count = sums[LC : LC + 8, :]
    moments = [rho * sums[LF + 8 * k : LF + 8 * k + 8, :] for k in range(4)]
    moments[2] = 0.7 * moments[2] + 0.3 * rho * temp0 * count
    later = [rates(blocks, mid[NS + NB * t : NS + NB * (t + 1), :]) for t in range(2)]

    def current(b):
        return [mid[NS * b : NS * (b + 1), NB * h : NB * (h + 1)] for h in range(2)]

    def reaction(r):
        return [later[r // 4][NS * (r % 4) : NS * (r % 4 + 1), NB * h : NB * (h + 1)] for h in range(2)]

    released = jnp.concatenate([x[NB : NB + 4] for x in later], axis=0)

    def put(r, new):
        turned[r // 4, NS * (r % 4) : NS * (r % 4 + 1), :] = new[0]

    rho, temp1 = advance(rho * count, moments, 8 * me, current, reaction, released, put)

    own = section_lane(got[row_at // 2, 0:C, LOWN : LOWN + 1], core)
    own = jnp.concatenate([own] * 3 + [jnp.full((NB - 3 * C, 1), -1, jnp.int32)], axis=0)
    hot = jnp.where(own == iota((NB, SECT), 1), 1.0, 0.0).astype(BF16)
    table = jnp.concatenate([temp0, temp1, rho], axis=0)
    full = dot(jnp.concatenate(parts(table), axis=0), hot, ((1,), (1,)))
    full = full[0:24] + full[24:48] + full[48:72]
    lane = iota((8, NB), 1)
    cells = jnp.where(lane < C, full[0:8], jnp.where(lane < 2 * C, full[8:16], full[16:24]))
    for t in range(2):
        turned[t] = turned[t].T
    lane = iota((G, NB), 1)
    start = pl.multiple_of(16 * (row_at // 2), 16)
    for b in range(8):
        own_sections = turned[b // 4, pl.ds(start, G), :]
        moved = pltpu.roll(own_sections, (96 - 32 * (b % 4)) % NB, 1)
        out[pl.ds(b, G, stride=8), :] = jnp.where(lane >= 96, moved, cells[b : b + 1, :])


def cell_kernel(got, halo, bins, once, early, species_to, density_to, fields_to, species_out, density_out, field, left_at):
    leaving = []

    def leave(source, to):
        leaving.append(pltpu.make_async_copy(source, to, left_at.at[len(leaving)]))
        leaving[-1].start()

    for n, k in enumerate((0, 1, 3)):
        leave(early.at[n], fields_to.at[k])
    table = got[...].reshape(NB, NB).T
    temp0, temp1, rho = table[0:C], table[C : 2 * C], table[2 * C : 3 * C]
    index = [bins[:, 0:NB], bins[:, NB:Z], halo[4].astype(jnp.int32)]

    def look(tab, index):
        return jnp.take_along_axis(tab, index, axis=1)

    def relaxed(tiles, tab):
        return [t + 0.3 * (look(tab, i) - t) for t, i in zip(tiles, index)]

    species_out[0] = table[96:128]
    leave(species_out, species_to)
    for h in range(2):
        density_out[:, NB * h : NB * (h + 1)] = look(rho, index[h])
    leave(density_out, density_to)
    tiles = relaxed(diffused(relaxed([once[h] for h in range(3)], temp0)), temp1)
    for h in range(2):
        field[:, NB * h : NB * (h + 1)] = tiles[h]
    leave(field, fields_to.at[2])
    for copy in leaving:
        copy.wait()


def call(kernel, name, outs, ins, scratch=(), source=pltpu.VMEM):
    outs = [(pltpu.VMEM, jax.ShapeDtypeStruct(s, F32)) if isinstance(s[0], int) else s for s in outs]
    return pl.pallas_call(
        kernel,
        name=name,
        out_shape=[s if space == pltpu.VMEM else space(s.shape, s.dtype) for space, s in outs],
        in_specs=[pl.BlockSpec(memory_space=source)] * len(ins),
        out_specs=[pl.BlockSpec(memory_space=space) for space, _ in outs],
        scratch_shapes=[pltpu.VMEM(s, F32) if isinstance(s, tuple) else s for s in scratch],
        compiler_params=pltpu.CompilerParams(vmem_limit_bytes=16 << 20),
    )(*ins)


def body(density, fields, bins, owner, species, rate_matrix, inv_weight, formation):
    dma = pltpu.SemaphoreType.DMA
    ins = [bins, density, fields, owner.reshape(1, C)]
    ins += [species, rate_matrix, inv_weight.reshape(1, NS), formation.reshape(1, NS)]
    sent, consts = call(
        bin_kernel,
        "bin",
        [(G, C, NB), (NS, NB)],
        [pltpu.with_memory_space_constraint(x, pltpu.HBM) for x in ins],
        [pltpu.VMEM(x.shape, x.dtype) for x in ins]
        + [(2, 48 * C, NB), (16 * C, NB), (264, NB), (C, Z), dma((11,))],
        pltpu.HBM,
    )
    got = lax.all_to_all(sent, "span", 0, 0, tiled=True)
    sent, halo = call(column_kernel, "column", [(G // 2, R2, NB), (5, C, NB)], [got.reshape(G * C, NB)])
    groups = [list(range(core, G, 2)) for core in range(2)]
    got = lax.all_to_all(sent, "sec", 0, 0, axis_index_groups=groups, tiled=True)
    other = lax.ppermute(got, "sec", [(i, i ^ 1) for i in range(G)])
    halves = [(NB, SECT), (3, NB, NB), (3, NB + 8, NB)]
    blocks = (pltpu.VMEM, jax.ShapeDtypeStruct((NB + 16, 2 * NB), BF16))
    far = [(pltpu.HBM, jax.ShapeDtypeStruct(s, F32)) for s in ((1, NS, NB), (C, Z), (4, C, Z))]
    *own, once, early = call(
        own_kernel, "own", halves + [blocks, (3, C, NB), (3, C, Z)], [got, consts, halo, fields]
    )
    scratch = halves + [(10 * NS, SECT), (2, NB, NB), (64, SECT)]
    (sent,) = call(section_kernel, "section", [(NB, NB)], [got, other, consts] + own, scratch)
    got = lax.all_to_all(sent.reshape(G, 8, NB), "span", 0, 0, tiled=True)
    scratch = [(1, NS, NB), (C, Z), (C, Z), dma((6,))]
    return call(cell_kernel, "cell", far, [got, halo, bins, once, early], scratch)


def solution(mesh):
    return jax.shard_map(
        lambda *args: tuple(body(*args)),
        mesh=mesh,
        in_specs=(
            P("sec", "span"),
            P(None, "sec", "span"),
            P("sec", "span"),
            P("sec"),
            P(("sec", "span"), None, None),
            P(),
            P(),
            P(),
        ),
        out_specs=(P(("sec", "span"), None, None), P("sec", "span"), P(None, "sec", "span")),
        check_vma=False,
    )
```

```python
import jax
import jax.numpy as jnp
from jax import lax
from jax.experimental import pallas as pl
from jax.experimental.pallas import tpu as pltpu
from jax.sharding import PartitionSpec as P

F32, BF16 = jnp.float32, jnp.bfloat16
C, Z, NB, NS = 24, 256, 128, 32
G = 16
SECT = 256
LF, LC, LH, LE = 0, 32, 40, 90
LB0, LB1, LOWN = 106, 107, 108
LS = 112
R2 = C + 3 * G


def iota(shape, dim):
    return lax.broadcasted_iota(jnp.int32, shape, dim)


def parts(value):
    high = value.astype(BF16)
    rest = value - high.astype(F32)
    mid = rest.astype(BF16)
    low = (rest - mid.astype(F32)).astype(BF16)
    return high, mid, low


def column_of(row, n):
    return jnp.sum(jnp.where(iota((n, n), 0) == iota((n, n), 1), row, 0.0), axis=1, keepdims=True)


def sigmoid(x):
    return 0.5 * jnp.tanh(0.5 * x) + 0.5


def dot(a, b, dims):
    return lax.dot_general(a, b, (dims, ((), ())), preferred_element_type=F32)


def bin_kernel(*refs):
    ins, (out, shared), held = refs[0:8], refs[8:10], refs[10:18]
    vals, hist, rows, labels, arrived = refs[18:23]
    bins, den, fields, owner, species, rate_matrix, inv_weight, formation = held
    moves = [(ins[n], held[n]) for n in (0, 1, 3, 4, 5, 6, 7)]
    moves += [(ins[2].at[k], held[2].at[k]) for k in range(4)]
    copies = [pltpu.make_async_copy(source, to, arrived.at[n]) for n, (source, to) in enumerate(moves)]
    for copy in copies:
        copy.start()

    def keep(q, value):
        high, mid, low = parts(value)
        for p, part in enumerate((high, mid, low)):
            at = C * (16 * p + q)
            part = part.astype(F32)
            vals[0, at : at + C, :] = part[:, 0:NB]
            vals[1, at : at + C, :] = part[:, NB:Z]

    keep(5, jnp.ones((C, Z), F32))
    for p in range(3):
        at = C * (16 * p + 10)
        for h in range(2):
            vals[h, at : at + 6 * C, :] = jnp.zeros((6 * C, NB), F32)
    rows[0:8, :] = jnp.zeros((8, NB), F32)
    rows[256:264, :] = jnp.zeros((8, NB), F32)
    for copy in copies:
        copy.wait()
    lane = iota((NS, NB), 1)
    block = jnp.concatenate([rate_matrix[...], jnp.zeros((NS, NB - NS), F32)], axis=1)
    block = jnp.where(lane == NS, column_of(inv_weight[...], NS), block)
    shared[...] = jnp.where(lane == NS + 1, column_of(formation[...], NS), block)
    lane = iota((C, Z), 1)
    d = den[...]

    keep(0, d)
    for k in range(4):
        f = fields[k]
        before = jnp.where(lane == 0, 0.0, pltpu.roll(f, 1, 1))
        after = jnp.where(lane == Z - 1, 0.0, pltpu.roll(f, Z - 1, 1))
        keep(1 + k, d * f)
        keep(6 + k, f + 0.2 * (before + after - 2.0 * f))
    labels[...] = bins[...].astype(F32)
    which = iota((NB, Z), 0).astype(F32).astype(BF16).reshape(8, 16, Z)
    one, zero = jnp.ones((8, 16, Z), BF16), jnp.zeros((8, 16, Z), BF16)
    for c in range(C):
        label = jnp.broadcast_to(labels[c : c + 1, :], (16, Z)).astype(BF16)
        hot = jnp.where(which == label[None], one, zero).reshape(NB, Z)
        cells = [vals[h, pl.ds(c, 48, stride=C), :] for h in range(2)]
        full = dot(jnp.concatenate(cells, axis=1).astype(BF16), hot, ((1,), (1,)))
        hist[16 * c : 16 * c + 16, :] = full[0:16] + full[16:32] + full[32:48]
    lane = iota((C, NB), 1)
    edge = jnp.zeros((C, NB), F32)
    for k in range(4):
        first, last = fields[k, :, 0:NB], fields[k, :, Z - NB : Z]
        for e, (tile, at) in enumerate(((first, 0), (first, 1), (last, NB - 2), (last, NB - 1))):
            to = LE + 4 * k + e
            edge = jnp.where(lane == to, pltpu.roll(tile, (to - at) % NB, 1), edge)
    first, last = labels[:, 0:NB], labels[:, Z - NB : Z]
    edge = jnp.where(lane == LB0, pltpu.roll(first, LB0, 1), edge)
    edge = jnp.where(lane == LB1, pltpu.roll(last, (LB1 + 1) % NB, 1), edge)
    edge = jnp.where(lane == LOWN, column_of(owner[...].astype(F32), C), edge)
    sums = [hist[pl.ds(q, C, stride=16), :] for q in range(10)]
    turned = jnp.concatenate([species[0], jnp.zeros((NB - NS, NB), F32)], axis=0).T
    rows[pl.ds(4, NB, stride=2), :] = pltpu.roll(turned, LS, 1)
    rows[pl.ds(5, NB, stride=2), :] = pltpu.roll(turned, LS - 16, 1)
    layout = [(LF + 8 * k, 0, 6 + k) for k in range(4)] + [(LC, 0, 5)] + [(LH + 10 * q, -1, q) for q in range(5)]
    turned = [pltpu.roll(sums[q], (start - at) % NB, 1) if start != at else sums[q] for start, at, q in layout]
    for dest in range(G):
        place = lane if dest == 0 else (lane - 8 * dest) & (NB - 1)
        acc = turned[0]
        for n in range(1, 10):
            acc = jnp.where(place >= layout[n][0], turned[n], acc)
        if dest:
            acc = pltpu.roll(acc, NB - 8 * dest, 1)
        acc = jnp.where(lane >= LE, edge, acc)
        acc = jnp.where(lane >= LS, rows[16 * dest : 16 * dest + C, :], acc)
        out[dest] = acc


def column_kernel(got, out, halo):
    me = lax.axis_index("span")
    lane = iota((C, NB), 1)
    total = got[0:C, :]
    for j in range(1, G):
        total = total + got[C * j : C * (j + 1), :]
    source, to = iota((NB, 2 * NB), 0), iota((NB, 2 * NB), 1)
    pick = jnp.where(
        to < 32,
        LE + 3 + 4 * (to // 8),
        jnp.where(
            to < 64,
            LE + 4 * ((to - 32) // 8),
            jnp.where((to >= 128) & (to < 160), LB0, jnp.where((to >= 160) & (to < 192), LB1, -1)),
        ),
    )
    spread = jnp.where(source == pick, 1.0, 0.0).astype(BF16)
    high, mid, low = parts(got[...])
    moved = dot(high, spread, ((1,), (0,))) + dot(mid, spread, ((1,), (0,))) + dot(low, spread, ((1,), (0,)))
    bin_here = (8 * me + lane % 8).astype(F32)
    part = [moved[C * j : C * (j + 1), 0:NB] for j in range(G)]
    fix = jnp.zeros((C, NB), F32)
    for j in range(G):
        beside = jnp.where(lane < 32, part[(j - 1) % G], part[(j + 1) % G])
        fix = fix + jnp.where(moved[C * j : C * (j + 1), NB : 2 * NB] == bin_here, beside, 0.0)
    fix = fix + pltpu.roll(fix, NB - 32, 1)
    total = total + jnp.where(lane < 32, 0.2 * fix, 0.0)
    total = jnp.where(lane >= LE, got[0:C, :], total)
    lane = iota((G, NB), 1)
    tiles = []
    for t in range(3):
        tile = jnp.zeros((G, NB), F32)
        for p in range(8):
            moved = pltpu.roll(got[pl.ds(8 * t + p, G, stride=C), :], (16 * p - LS) % NB, 1)
            tile = jnp.where((lane >= 16 * p) & (lane < 16 * p + 16), moved, tile)
        tiles.append(tile)
    for i in range(G // 2):
        out[i, 0:C, :] = total
        for t in range(3):
            out[i, C + G * t : C + G * (t + 1), :] = tiles[t]
    lane = iota((C, NB), 1)
    left = got[pl.ds(pl.multiple_of(C * lax.rem(me + G - 1, G), 8), C), :]
    right = got[pl.ds(pl.multiple_of(C * lax.rem(me + 1, G), 8), C), :]
    for k in range(4):
        first, last = pltpu.roll(right, NB - LE - 4 * k, 1), pltpu.roll(left, NB - LE - 4 * k - 4, 1)
        halo[k] = jnp.where(lane < 2, first, jnp.where(lane >= NB - 2, last, 0.0))
    first, last = pltpu.roll(right, NB - LB0, 1), pltpu.roll(left, NB - 1 - LB1, 1)
    halo[4] = jnp.where(lane == 0, first, jnp.where(lane == NB - 1, last, 0.0))


def section_lane(owner, core):
    owner = owner.astype(jnp.int32)
    return (owner >> 5) * 16 + (owner & 15) + jnp.where(((owner >> 4) & 1) == core, 0, NB)


def rates(blocks, tile):
    high = tile.astype(BF16)
    mid = (tile - high.astype(F32)).astype(BF16)
    pair = dot(blocks[:, 0 : 2 * NB], jnp.concatenate([high, high], axis=0), ((1,), (0,)))
    return (pair + dot(blocks[:, 0:NB], mid, ((1,), (0,))))[0 : NB + 8]


def half_sums(got, core, blocks, species, reacts):
    wide = got[:, 0:C, :].reshape(G // 2 * C, NB)
    lane = section_lane(wide[:, LOWN : LOWN + 1], core)
    hot = jnp.where(lane == iota((G // 2 * C, SECT), 1), 1.0, 0.0).astype(BF16)
    full = dot(jnp.concatenate(parts(wide.T), axis=0), hot, ((1,), (0,)))
    for t in range(3):
        tile = got[:, C + G * t : C + G * (t + 1), :].reshape(NB, NB).T
        species[t] = tile
        reacts[t] = rates(blocks, tile)
    return full[0:NB] + full[NB : 2 * NB] + full[2 * NB : 3 * NB]


def diffused(tiles):
    first, last = iota((C, NB), 1) == 0, iota((C, NB), 1) == NB - 1
    up, down = [pltpu.roll(t, 1, 1) for t in tiles], [pltpu.roll(t, NB - 1, 1) for t in tiles]
    return [
        t + 0.2 * (jnp.where(first, up[n - 1], up[n]) + jnp.where(last, down[(n + 1) % 3], down[n]) - 2.0 * t)
        for n, t in enumerate(tiles)
    ]


def own_kernel(got, consts, halo, fields, sums, species, reacts, blocks, once, early):
    for n, k in enumerate((0, 1, 3, 2)):
        tiles = diffused([fields[k, :, 0:NB], fields[k, :, NB:Z], halo[k]])
        if k == 2:
            for h in range(3):
                once[h] = tiles[h]
            continue
        tiles = diffused(tiles)
        for h in range(2):
            early[n, :, NB * h : NB * (h + 1)] = tiles[h]
    block = jnp.concatenate([consts[:, 0:NS]] * 4, axis=1)
    block = jnp.concatenate([block] * 4, axis=0)
    released = jnp.sum(consts[:, NS + 1 : NS + 2] * consts[:, 0:NS], axis=0, keepdims=True)
    block = jnp.concatenate([block, jnp.concatenate([jnp.broadcast_to(released, (8, NS))] * 4, axis=1)], axis=0)
    row = iota((NB + 8, NB), 0)
    block = jnp.where(jnp.where(row < NB, row // NS, row - NB) == iota((NB + 8, NB), 1) // NS, block, 0.0)
    high, mid, _ = parts(block)
    blocks[0 : NB + 8, 0:NB] = high
    blocks[0 : NB + 8, NB : 2 * NB] = mid
    blocks[NB + 8 : NB + 16, :] = jnp.zeros((8, 2 * NB), BF16)
    core = lax.rem(lax.axis_index("sec"), 2)
    sums[...] = half_sums(got, core, blocks, species, reacts)


def section_kernel(got, other, consts, own_sums, own_species, own_reacts, blocks, out, sums, species, reacts, mid, turned, rows_of):
    row_at, me = lax.axis_index("sec"), lax.axis_index("span")
    core = lax.rem(row_at, 2)
    sums[...] = own_sums[...] + half_sums(other, core, blocks, species, reacts)
    weights = consts[:, NS : NS + 1]
    lane = iota((NS, NB), 1)
    starts = (lane & 15) == 0
    section_0 = iota((1, SECT), 1) == NB * core
    near, far = jnp.where(core == 0, 1, NB - 15), jnp.where(core == 0, NB - 15, 1)

    def advance(density, moments, bin_at, current, reaction, released, put):
        n = density.shape[0]
        inner = slice(1, 9) if n == 10 else slice(0, 8)
        weight = jnp.maximum(density, 1.0)
        cond = [m / weight for m in moments]
        eta = ((bin_at + iota((n, SECT), 0)).astype(F32) + 0.5) / NB
        temp = 1.0 + 4.0 * eta * (1.0 - eta) + 0.5 * jnp.tanh(cond[2])
        rate = jnp.exp(2.0 * (1.0 - 1.0 / temp))
        mixing = 0.2 * sigmoid(cond[1])
        carried = 0.3 * sigmoid(cond[0])
        follow = jnp.where(section_0, 0.0, carried)
        for c, coefficient in enumerate((1.0 - 2.0 * mixing - carried, mixing, follow, 0.2 * rate)):
            rows_of[16 * c : 16 * c + n, :] = coefficient
        mixes = []
        for r in range(n):
            here = current(r + 1)
            above, below, react = current(r + 2), current(r), reaction(r)
            before = (
                jnp.where(starts, pltpu.roll(here[1], near, 1), pltpu.roll(here[0], 1, 1)),
                jnp.where(starts, pltpu.roll(here[0], far, 1), pltpu.roll(here[1], 1, 1)),
            )
            new = []
            for h in range(2):
                half = slice(NB * h, NB * (h + 1))
                keep, spread, follow, grow = [rows_of[16 * c + r : 16 * c + r + 1, half] for c in range(4)]
                new.append(keep * here[h] + spread * (above[h] + below[h]) + follow * before[h] + grow * react[h])
            put(r, new)
            if inner.start <= r < inner.stop:
                mixes.append(
                    jnp.concatenate([jnp.sum(weights * x * x, axis=0, keepdims=True) for x in new], axis=1)
                )
        mix = 1.0 + jnp.concatenate(mixes, axis=0) / NS
        temp, rate, loss = temp[inner], rate[inner], cond[3][inner]
        rho = 1.0 / (temp * mix)
        temp_c = temp + 0.1 * rate * released - 0.2 * sigmoid(loss) * (temp - 0.5)
        return rho, temp_c

    def current(b):
        rows = slice(NS * (b % 4), NS * (b % 4 + 1))
        return own_species[b // 4, rows, :], species[b // 4, rows, :]

    def reaction(r):
        rows = slice(NS * ((r + 1) % 4), NS * ((r + 1) % 4 + 1))
        return own_reacts[(r + 1) // 4, rows, :], reacts[(r + 1) // 4, rows, :]

    released = [[x[t, NB : NB + 4, :] for t in range(3)] for x in (own_reacts, reacts)]
    released = jnp.concatenate([jnp.concatenate(x, axis=0)[2:10] for x in released], axis=1)
    first = [sums[LH + 10 * q : LH + 10 * (q + 1), :] for q in range(5)]

    def put(r, new):
        outside = (me == 0) if r == 0 else (me == G - 1) if r == 9 else None
        for h in range(2):
            value = new[h] if outside is None else jnp.where(outside, 0.0, new[h])
            mid[NS * r : NS * (r + 1), NB * h : NB * (h + 1)] = value

    rho, temp0 = advance(first[0], first[1:], 8 * me - 1, current, reaction, released, put)
    count = sums[LC : LC + 8, :]
    moments = [rho * sums[LF + 8 * k : LF + 8 * k + 8, :] for k in range(4)]
    moments[2] = 0.7 * moments[2] + 0.3 * rho * temp0 * count
    later = [rates(blocks, mid[NS + NB * t : NS + NB * (t + 1), :]) for t in range(2)]

    def current(b):
        return [mid[NS * b : NS * (b + 1), NB * h : NB * (h + 1)] for h in range(2)]

    def reaction(r):
        return [later[r // 4][NS * (r % 4) : NS * (r % 4 + 1), NB * h : NB * (h + 1)] for h in range(2)]

    released = jnp.concatenate([x[NB : NB + 4] for x in later], axis=0)

    def put(r, new):
        turned[r // 4, NS * (r % 4) : NS * (r % 4 + 1), :] = new[0]

    rho, temp1 = advance(rho * count, moments, 8 * me, current, reaction, released, put)

    own = section_lane(got[row_at // 2, 0:C, LOWN : LOWN + 1], core)
    own = jnp.concatenate([own] * 3 + [jnp.full((NB - 3 * C, 1), -1, jnp.int32)], axis=0)
    hot = jnp.where(own == iota((NB, SECT), 1), 1.0, 0.0).astype(BF16)
    table = jnp.concatenate([temp0, temp1, rho], axis=0)
    full = dot(jnp.concatenate(parts(table), axis=0), hot, ((1,), (1,)))
    full = full[0:24] + full[24:48] + full[48:72]
    lane = iota((8, NB), 1)
    cells = jnp.where(lane < C, full[0:8], jnp.where(lane < 2 * C, full[8:16], full[16:24]))
    for t in range(2):
        turned[t] = turned[t].T
    lane = iota((G, NB), 1)
    start = pl.multiple_of(16 * (row_at // 2), 16)
    for b in range(8):
        own_sections = turned[b // 4, pl.ds(start, G), :]
        moved = pltpu.roll(own_sections, (96 - 32 * (b % 4)) % NB, 1)
        out[pl.ds(b, G, stride=8), :] = jnp.where(lane >= 96, moved, cells[b : b + 1, :])


def cell_kernel(got, halo, bins, once, early, species_to, density_to, fields_to, species_out, density_out, field, left_at):
    leaving = []

    def leave(source, to):
        leaving.append(pltpu.make_async_copy(source, to, left_at.at[len(leaving)]))
        leaving[-1].start()

    for n, k in enumerate((0, 1, 3)):
        leave(early.at[n], fields_to.at[k])
    table = got[...].reshape(NB, NB).T
    temp0, temp1, rho = table[0:C], table[C : 2 * C], table[2 * C : 3 * C]
    index = [bins[:, 0:NB], bins[:, NB:Z], halo[4].astype(jnp.int32)]

    def look(tab, index):
        return jnp.take_along_axis(tab, index, axis=1)

    def relaxed(tiles, tab):
        return [t + 0.3 * (look(tab, i) - t) for t, i in zip(tiles, index)]

    tiles = relaxed(diffused(relaxed([once[h] for h in range(3)], temp0)), temp1)
    for h in range(2):
        field[:, NB * h : NB * (h + 1)] = tiles[h]
    leave(field, fields_to.at[2])
    species_out[0] = table[96:128]
    leave(species_out, species_to)
    for h in range(2):
        density_out[:, NB * h : NB * (h + 1)] = look(rho, index[h])
    leave(density_out, density_to)
    for copy in leaving:
        copy.wait()


def call(kernel, name, outs, ins, scratch=(), source=pltpu.VMEM):
    outs = [(pltpu.VMEM, jax.ShapeDtypeStruct(s, F32)) if isinstance(s[0], int) else s for s in outs]
    return pl.pallas_call(
        kernel,
        name=name,
        out_shape=[s if space == pltpu.VMEM else space(s.shape, s.dtype) for space, s in outs],
        in_specs=[pl.BlockSpec(memory_space=source)] * len(ins),
        out_specs=[pl.BlockSpec(memory_space=space) for space, _ in outs],
        scratch_shapes=[pltpu.VMEM(s, F32) if isinstance(s, tuple) else s for s in scratch],
        compiler_params=pltpu.CompilerParams(vmem_limit_bytes=16 << 20),
    )(*ins)


def body(density, fields, bins, owner, species, rate_matrix, inv_weight, formation):
    dma = pltpu.SemaphoreType.DMA
    ins = [bins, density, fields, owner.reshape(1, C)]
    ins += [species, rate_matrix, inv_weight.reshape(1, NS), formation.reshape(1, NS)]
    sent, consts = call(
        bin_kernel,
        "bin",
        [(G, C, NB), (NS, NB)],
        [pltpu.with_memory_space_constraint(x, pltpu.HBM) for x in ins],
        [pltpu.VMEM(x.shape, x.dtype) for x in ins]
        + [(2, 48 * C, NB), (16 * C, NB), (264, NB), (C, Z), dma((11,))],
        pltpu.HBM,
    )
    got = lax.all_to_all(sent, "span", 0, 0, tiled=True)
    sent, halo = call(column_kernel, "column", [(G // 2, R2, NB), (5, C, NB)], [got.reshape(G * C, NB)])
    groups = [list(range(core, G, 2)) for core in range(2)]
    got = lax.all_to_all(sent, "sec", 0, 0, axis_index_groups=groups, tiled=True)
    other = lax.ppermute(got, "sec", [(i, i ^ 1) for i in range(G)])
    halves = [(NB, SECT), (3, NB, NB), (3, NB + 8, NB)]
    blocks = (pltpu.VMEM, jax.ShapeDtypeStruct((NB + 16, 2 * NB), BF16))
    far = [(pltpu.HBM, jax.ShapeDtypeStruct(s, F32)) for s in ((1, NS, NB), (C, Z), (4, C, Z))]
    *own, once, early = call(
        own_kernel, "own", halves + [blocks, (3, C, NB), (3, C, Z)], [got, consts, halo, fields]
    )
    scratch = halves + [(10 * NS, SECT), (2, NB, NB), (64, SECT)]
    (sent,) = call(section_kernel, "section", [(NB, NB)], [got, other, consts] + own, scratch)
    got = lax.all_to_all(sent.reshape(G, 8, NB), "span", 0, 0, tiled=True)
    scratch = [(1, NS, NB), (C, Z), (C, Z), dma((6,))]
    return call(cell_kernel, "cell", far, [got, halo, bins, once, early], scratch)


def solution(mesh):
    return jax.shard_map(
        lambda *args: tuple(body(*args)),
        mesh=mesh,
        in_specs=(
            P("sec", "span"),
            P(None, "sec", "span"),
            P("sec", "span"),
            P("sec"),
            P(("sec", "span"), None, None),
            P(),
            P(),
            P(),
        ),
        out_specs=(P(("sec", "span"), None, None), P("sec", "span"), P(None, "sec", "span")),
        check_vma=False,
    )
```
